256 devices in a mesh: expert: 32 (over x, y, core), group: 8 (over z).
Axes of the slice: x: 4, y: 4, z: 8, core: 2. Of those that a mesh axis runs over, the one named last changes fastest.
Arguments:
- tokens: bfloat16 [2048, 7168], P(('expert', 'group')), may hold values from -6 to 6
- routes: int32 [2048, 8], P(('expert', 'group')), may hold values from 0 to 31, all different within a row; in each aligned block of 8 rows (0 to 7, 8 to 15, ...) at most 4 rows name the same one
- gate_weight: bfloat16 [32, 7168, 2048], P('expert', None, 'group'), may hold values from -0.0625 to 0.0625
- up_weight: bfloat16 [32, 7168, 2048], P('expert', None, 'group'), may hold values from -0.0625 to 0.0625
- down_weight: bfloat16 [32, 2048, 7168], P('expert', 'group'), may hold values from -6 to 6
- merge_group: int32 [32], replicated, may hold values from 0 to 7, as said below
- neuron_perm: int32 [32, 2048], P('expert', 'group'), may hold values from 0 to 2047, as said below
Outputs:
- merged_down: bfloat16 [8, 2048, 7168], P(None, 'group', 'expert')
The draws below stay inside these ranges and needn't reach their ends.
Inputs may be any that keep to these rules, and one draw needn't show every extreme that they name: `routes`: among the rows of one device (8 rows), no expert is named by more than 4 rows. `merge_group`: every one of the 8 merge groups has at least one expert. `neuron_perm`: each row is a permutation of 0 to 2047 that keeps every hidden unit within its aligned block of 128.
All inputs are finite; a program needn't handle non-finite values.
Results may differ from the reference program's by a relative error of at most 0.0047.
Values may be sent and summed in bfloat16 or wider, within the bound.
A program may use at most 128 MiB of HBM per device.

```python
import math
import jax
import jax.numpy as jnp
import numpy as np
from jax import lax

D = 7168
FFW = 2048
TOP = 8
NB = 128
TOK_DEV = 8
EXPERTS = 32
MGROUPS = 8
CAP = 4
TOKENS = 2048
DEVICES = 256


def draw_merge_group(key, part):
    shuffle = jax.random.permutation(jax.random.fold_in(key, 11), EXPERTS)
    draw_one = jax.random.randint(jax.random.fold_in(key, 12), (EXPERTS,), 0, MGROUPS)
    draw_two = jax.random.randint(jax.random.fold_in(key, 13), (EXPERTS,), 0, MGROUPS)
    leftover = jnp.minimum(draw_one, draw_two)
    placed = jnp.arange(EXPERTS, dtype=jnp.int32)
    values = jnp.where(placed < MGROUPS, placed, leftover).astype(jnp.int32)
    return jnp.zeros((EXPERTS,), jnp.int32).at[shuffle].set(values)


def draw_neuron_perm(key, part):
    block_count = FFW // NB
    scores = jax.random.randint(jax.random.fold_in(key, 21), (EXPERTS, block_count, NB), 0, 2 ** 20)
    scores = scores * NB + jnp.arange(NB, dtype=jnp.int32)[None, None, :]
    within = jnp.argsort(scores, axis=-1).astype(jnp.int32)
    offsets = (jnp.arange(block_count, dtype=jnp.int32) * NB)[None, :, None]
    return (within + offsets).reshape(EXPERTS, FFW)


def levels(stream_key, extent, pieces, low, top_value):
    level, own = 1.0, jax.random.fold_in(stream_key, 6)
    for dim, parts in pieces:
        heights = jnp.exp(jax.random.uniform(jax.random.fold_in(own, dim), (parts,), jnp.float32, low / len(pieces), top_value / len(pieces)))
        level = level * jnp.repeat(heights, extent[dim] // parts).reshape([-1 if axis == dim else 1 for axis in range(len(extent))])
    return level


def shared_out(key, own, number, rows, amount, top, reach, slope):
    sequence = jax.random.permutation(key, amount)
    packed, common = portions_of(amount, rows * top, reach, slope, True), portions_of(amount, rows * top, reach, slope, False)
    places = jnp.arange(amount)

    def named(sizes, rotation):
        used = int((sizes > 0).sum())
        fixed = max(1, used // 4)
        passed = fixed + (places - fixed + rotation * (used - fixed)) % max(1, amount - fixed)
        return jnp.zeros((amount,), jnp.int32).at[sequence[jnp.where(places < fixed, places, passed)]].set(jnp.asarray(sizes, jnp.int32))

    sizes = jnp.where(number % 4 == 0, named(packed, number // 4), named(common, number - number // 4 - 1))
    mixed = jax.random.permutation(jax.random.fold_in(own, 3), amount)
    donor, receiver = mixed[0:amount // 2 * 2:2], mixed[1:amount // 2 * 2:2]
    margin = jnp.minimum(sizes[donor] - 1, reach - sizes[receiver]) // 2
    margin = jnp.where((donor == sequence[0]) | (receiver == sequence[0]) | (sizes[receiver] == 0), 0, jnp.maximum(margin, 0))
    passed = jax.random.randint(jax.random.fold_in(own, 4), (amount // 2,), 0, 1 << 20) % (margin + 1)
    sizes = sizes.at[donor].add(-passed).at[receiver].add(passed)
    members = jnp.searchsorted(jnp.cumsum(sizes), jnp.arange(rows * top), side="right").astype(jnp.int32)
    table = members.reshape(top, rows).T
    table = table[jax.random.permutation(jax.random.fold_in(own, 1), rows)]
    rotation = jax.random.randint(jax.random.fold_in(own, 2), (rows, 1), 0, top)
    return jnp.take_along_axis(table, (jnp.arange(top)[None, :] + rotation) % top, axis=1)


def portions_of(count, total, reach, skew, full):
    portions = [(1 << 20) // math.isqrt(grade ** skew) + 1 for grade in range(1, count + 1)]
    largest = reach if full else min(reach, max(-(-total // count), total * portions[0] // sum(portions)))
    least = 1 if total - largest >= count - 1 else 0
    given, spare = [largest] + [least] * (count - 1), total - largest - least * (count - 1)
    while spare > 0:
        movable = [i for i in range(1, count) if given[i] < largest] or [i for i in range(1, count) if given[i] < reach]
        whole, remaining = sum([portions[i] for i in movable]), spare
        for i in movable:
            extra = min(reach - given[i], max(1, remaining * portions[i] // whole), spare)
            given[i] = given[i] + extra
            spare = spare - extra
    return np.array(given)


def normal_values(stream_key, dims, width, limit, shards=(), kind=jnp.bfloat16):
    level = levels(stream_key, dims, shards, -0.22, 0.18) if shards else 1.0
    entries = jax.random.normal(stream_key, dims, jnp.float32) * width * level
    return jnp.minimum(jnp.maximum(entries, -limit), limit).astype(kind)


def setup_inputs(seed: int = 0) -> dict:
    arg_keys = jax.random.split(jax.random.key(seed), 8)
    tokens = normal_values(arg_keys[0], (TOKENS, D), 1.0, 6.0, ((0, 256),))
    routes_keys = jax.random.split(jax.random.fold_in(arg_keys[1], 1), TOKENS // TOK_DEV)
    routes_turns = jax.random.permutation(jax.random.fold_in(arg_keys[1], 3), TOKENS // TOK_DEV)
    routes = jax.vmap(lambda own, number: shared_out(jax.random.fold_in(arg_keys[1], 2), own, number, TOK_DEV, EXPERTS, TOP, CAP, 2))(routes_keys, routes_turns).reshape((TOKENS, TOP))
    gate_weight = normal_values(arg_keys[2], (EXPERTS, D, FFW), D ** -0.5, 0.0625, ((0, 32), (2, 8)))
    up_weight = normal_values(arg_keys[3], (EXPERTS, D, FFW), D ** -0.5, 0.0625, ((0, 32), (2, 8)))
    down_weight = normal_values(arg_keys[4], (EXPERTS, FFW, D), 1.0, 6.0, ((0, 32), (1, 8)))
    merge_group = draw_merge_group(jax.random.fold_in(arg_keys[7], 71), 0)
    neuron_perm = draw_neuron_perm(jax.random.fold_in(arg_keys[7], 71), 0)
    return dict(tokens=tokens, routes=routes, gate_weight=gate_weight, up_weight=up_weight, down_weight=down_weight, merge_group=merge_group, neuron_perm=neuron_perm)


off_weight = 0.75
ridge_eps = 1e-05

def slot_lists(routes):
    blocks = routes.reshape(DEVICES, TOK_DEV * TOP)
    onehot = (blocks[:, :, None] == jnp.arange(EXPERTS, dtype=jnp.int32)[None, None, :]).astype(jnp.int32)
    position = jnp.sum((jnp.cumsum(onehot, axis=1) - 1) * onehot, axis=2).astype(jnp.int32)
    token_id = (jnp.arange(TOK_DEV * TOP, dtype=jnp.int32) // TOP)[None, :] + (jnp.arange(DEVICES, dtype=jnp.int32) * TOK_DEV)[:, None]
    slot_row = (jnp.arange(DEVICES, dtype=jnp.int32) * CAP)[:, None] + position
    listing = jnp.full((EXPERTS, DEVICES * CAP), -1, jnp.int32)
    return listing.at[blocks, slot_row].set(token_id.astype(jnp.int32))

def build_system(summed):
    unit_matrix = jnp.eye(summed.shape[-1], dtype=jnp.float32)
    return off_weight * summed + (1.0 - off_weight) * (summed * unit_matrix) + ridge_eps * unit_matrix

def apply_inverse(factor, right_side):
    forward = lax.linalg.triangular_solve(factor, right_side, left_side=True, lower=True)
    return lax.linalg.triangular_solve(factor, forward, left_side=True, lower=True, transpose_a=True)

def reference(tokens, routes, gate_weight, up_weight, down_weight, merge_group, neuron_perm):
    listing = slot_lists(routes)
    block_count = FFW // NB

    def one_expert(state_pair, expert_id):
        grams, terms = state_pair
        chosen = listing[expert_id]
        gathered = tokens[jnp.maximum(chosen, 0)]
        gathered = jnp.where((chosen >= 0)[:, None], gathered, jnp.zeros_like(gathered))
        gate_part = jnp.dot(gathered.astype(jnp.float32), gate_weight[expert_id].astype(jnp.float32), preferred_element_type=jnp.float32)
        up_part = jnp.dot(gathered.astype(jnp.float32), up_weight[expert_id].astype(jnp.float32), preferred_element_type=jnp.float32)
        hidden = (jax.nn.silu(gate_part) * up_part).astype(jnp.bfloat16)
        neuron_order = neuron_perm[expert_id]
        aligned = hidden[:, neuron_order].astype(jnp.float32).reshape(-1, block_count, NB)
        gram = jnp.einsum('sbi,sbk->bik', aligned, aligned, precision=lax.Precision.HIGHEST)
        moved_rows = down_weight[expert_id][neuron_order].astype(jnp.float32).reshape(block_count, NB, D)
        term_part = jnp.einsum('bni,bid->bnd', gram, moved_rows, precision=lax.Precision.HIGHEST)
        group_id = merge_group[expert_id]
        grams = grams.at[group_id].add(gram)
        terms = terms.at[group_id].add(term_part)
        return ((grams, terms), None)
    start_grams = jnp.zeros((MGROUPS, block_count, NB, NB), jnp.float32)
    start_terms = jnp.zeros((MGROUPS, block_count, NB, D), jnp.float32)
    (grams, terms), unused = lax.scan(one_expert, (start_grams, start_terms), jnp.arange(EXPERTS, dtype=jnp.int32))
    system = build_system(grams)
    factor = jnp.linalg.cholesky(system)
    merged = apply_inverse(factor, terms)
    return merged.reshape(MGROUPS, FFW, D).astype(jnp.bfloat16)
```

```python
from functools import partial

import jax
import jax.numpy as jnp
from jax import lax
from jax.experimental import pallas as pl
from jax.experimental.pallas import tpu as pltpu
from jax.sharding import PartitionSpec as P

NB = 128
F32 = jnp.float32
BF16 = jnp.bfloat16
MESH = pl.DeviceIdType.MESH
XN, YN, ZN = 4, 4, 8


def place(x, y, core):
    return (x * YN + y) * 2 + core


def gather_kernel(part, width, tok_ref, gate_ref, up_ref, out_ref, bufx, bufy, bufz, weights, acc, lhs,
                  send_sem, recv_sem, own_sem, wsem, wsend, wrecv):
    expert = lax.axis_index("expert")
    z = lax.axis_index("group")
    core = lax.rem(expert, 2)
    y = lax.rem(lax.div(expert, 2), YN)
    x = lax.div(expert, 2 * YN)
    units = gate_ref.shape[1]

    def device(axis, shift):
        px, py, pz, pc = x, y, z, core
        if axis == "x":
            px = lax.rem(x + XN + shift, XN)
        elif axis == "y":
            py = lax.rem(y + YN + shift, YN)
        elif axis == "z":
            pz = lax.rem(z + ZN + shift, ZN)
        else:
            pc = 1 - core
        return (place(px, py, pc), pz)

    colors = (
        (bufx, (("z", ZN, z), ("y", YN, y), ("x", XN, x)), (x, y)),
        (bufy, (("z", ZN, z), ("x", XN, x), ("y", YN, y)), (y, x)),
        (bufz, (("y", YN, y), ("x", XN, x), ("z", ZN, z)), (z, x)),
    )
    columns = (0, part, 2 * part)
    half_cols = (part // 256) * 128 + 128

    barrier = pltpu.get_barrier_semaphore()
    neighbours = [device(a, s) for a in "xyz" for s in (1, -1)] + [device("core", 0)]
    for other in neighbours:
        pl.semaphore_signal(barrier, inc=1, device_id=other, device_id_type=MESH)
    pl.semaphore_wait(barrier, len(neighbours))

    def unit(color, stage, pos, half=None):
        buf, _, (first, second) = colors[color]
        if stage == 0:
            if half is None:
                return buf.at[first, second, pos]
            cols = pl.ds(0, half_cols) if half == 0 else pl.ds(half_cols, part - half_cols)
            return buf.at[first, second, pos, :, cols]
        lead = (first, pos) if stage == 1 else (pos,)
        size = buf.shape[len(lead)]
        if half is not None:
            lead = lead + (pl.ds(half * (size // 2), size // 2),)
        return buf.at[lead]

    started = {}

    def start(color, stage, step):
        axis, n, pos = colors[color][1][stage]
        for way, sign in ((0, 1), (1, -1)):
            half = way if step == n // 2 else None
            which = lax.rem(pos + n - sign * (step - 1), n)
            dst = unit(color, stage, which, half)
            src = dst
            if stage == 0 and step == 1:
                src = tok_ref.at[:, pl.ds(columns[color], part)]
            copy = pltpu.make_async_remote_copy(
                src_ref=src,
                dst_ref=dst,
                send_sem=send_sem.at[color, stage, way, step - 1],
                recv_sem=recv_sem.at[color, stage, way, step - 1],
                device_id=device(axis, sign),
                device_id_type=MESH,
            )
            copy.start()
            started[color, stage, way, step] = copy

    def arrive(color, stage, step):
        for way in (0, 1):
            started[color, stage, way, step].wait_recv()

    for color in range(3):
        start(color, 0, 1)
    own = []
    for color in range(3):
        axis, n, pos = colors[color][1][0]
        copy = pltpu.make_async_copy(tok_ref.at[:, pl.ds(columns[color], part)], unit(color, 0, pos), own_sem.at[color])
        copy.start()
        own.append(copy)
    moves = []
    for j, ref in enumerate((gate_ref, up_ref)):
        local = pltpu.make_async_copy(ref, weights.at[core * 2 + j], wsem.at[j])
        local.start()
        remote = pltpu.make_async_remote_copy(
            src_ref=ref,
            dst_ref=weights.at[core * 2 + j],
            send_sem=wsend.at[j],
            recv_sem=wrecv.at[j],
            device_id=device("core", 0),
            device_id_type=MESH,
        )
        remote.start()
        moves.append((local, remote))
    acc[...] = jnp.zeros_like(acc)
    for copy in own:
        copy.wait()
    for step in range(1, 5):
        for color in (0, 1):
            arrive(color, 0, step)
            if step < 4:
                start(color, 0, step + 1)
            else:
                start(color, 1, 1)
        stage, sub = (0, step) if step <= 2 else (1, step - 2)
        arrive(2, stage, sub)
        if sub == 1:
            start(2, stage, 2)
        elif stage == 0:
            start(2, 1, 1)
        else:
            start(2, 2, 1)

    def multiply(plane_rows, depth, first_row, slot):
        def per_column(n, carry):
            w = weights[n, pl.ds(first_row, depth), :]
            value = jnp.dot(lhs[0:plane_rows, 0:depth], w, preferred_element_type=F32)
            if slot[0] == "x":
                acc[n, slot[1]] += value.reshape(YN, ZN, 8, units)
            elif slot[0] == "y":
                acc[n, :, slot[1]] += value.reshape(XN, ZN, 8, units)
            else:
                acc[n, :, :, slot[1]] += value.reshape(XN, YN, 8, units)
            return carry

        lax.fori_loop(0, 4, per_column, 0)

    def take(color, plane):
        buf = colors[color][0]
        depth = part if color < 2 else width - 2 * part
        rows = 256 if color < 2 else 128
        value = buf[plane, :, :, :, 0:depth].astype(F32)
        lhs[0:rows, 0:depth] = value.reshape(rows, depth).astype(BF16)
        multiply(rows, depth, columns[color], ("xyz"[color], plane))

    def near(axis, shift):
        n, pos = {"x": (XN, x), "y": (YN, y), "z": (ZN, z)}[axis]
        return lax.rem(pos + n + shift, n)

    for local, remote in moves:
        local.wait()
        remote.wait_recv()
    take(2, z)
    for color in (0, 1):
        arrive(color, 1, 1)
        start(color, 1, 2)
    for color in (0, 1):
        arrive(color, 1, 2)
        start(color, 2, 1)
    take(0, x)
    take(1, y)
    arrive(2, 2, 1)
    start(2, 2, 2)
    take(2, near("z", 1))
    take(2, near("z", -1))
    arrive(2, 2, 2)
    start(2, 2, 3)
    take(2, near("z", 2))
    take(2, near("z", -2))
    for color in (0, 1):
        arrive(color, 2, 1)
        start(color, 2, 2)
    take(0, near("x", 1))
    arrive(2, 2, 3)
    start(2, 2, 4)
    take(0, near("x", -1))
    take(1, near("y", 1))
    take(1, near("y", -1))
    take(2, near("z", 3))
    take(2, near("z", -3))
    arrive(2, 2, 4)
    take(2, near("z", 4))
    arrive(0, 2, 2)
    take(0, near("x", 2))
    arrive(1, 2, 2)
    take(1, near("y", 2))

    blocks = units // NB
    out_ref[...] = jnp.zeros_like(out_ref)
    spare = width - 2 * part

    def finish(i, carry):
        px, p = lax.div(i, 2), lax.rem(i, 2)
        named = (place(x, y, 0) + p).astype(F32)
        gate = acc[2 * p, px].reshape(256, units)
        up = acc[2 * p + 1, px].reshape(256, units)
        listed = jnp.concatenate(
            [bufz[:, px, py, :, spare : spare + NB].astype(F32).reshape(ZN * 8, NB) for py in range(YN)], axis=0
        )
        chosen = jnp.max(jnp.where(listed == named, 1.0, 0.0), axis=1, keepdims=True)
        value = gate / (1.0 + jnp.exp(-gate)) * up
        hidden = jnp.where(chosen > 0.5, value, 0.0).astype(BF16)
        for b in range(blocks):
            piece = hidden[:, b * NB : (b + 1) * NB]
            out_ref[p, b] += lax.dot_general(piece, piece, (((0,), (0,)), ((), ())), preferred_element_type=F32)
        return carry

    lax.fori_loop(0, 2 * XN, finish, 0)
    for copy in started.values():
        copy.wait_send()
    for _, remote in moves:
        remote.wait_send()


def gather_grams(tokens, routes, gate_weight, up_weight):
    rows, width = tokens.shape
    units = gate_weight.shape[1]
    listed = jnp.pad(routes.astype(BF16), ((0, 0), (0, NB - routes.shape[1])), constant_values=-1)
    wide = jnp.concatenate([tokens, listed], axis=1)
    part = (width + NB) // 3
    return pl.pallas_call(
        partial(gather_kernel, part, width),
        out_shape=jax.ShapeDtypeStruct((2, units // NB, NB, NB), F32),
        in_specs=[pl.BlockSpec(memory_space=pl.ANY)] * 3,
        out_specs=pl.BlockSpec(memory_space=pltpu.VMEM),
        scratch_shapes=[
            pltpu.VMEM((XN, YN, ZN, 8, part), BF16),
            pltpu.VMEM((YN, XN, ZN, 8, part), BF16),
            pltpu.VMEM((ZN, XN, YN, 8, part), BF16),
            pltpu.VMEM((4, width, units), BF16),
            pltpu.VMEM((4, XN, YN, ZN, 8, units), F32),
            pltpu.VMEM((256, part), BF16),
            pltpu.SemaphoreType.DMA((3, 3, 2, 4)),
            pltpu.SemaphoreType.DMA((3, 3, 2, 4)),
            pltpu.SemaphoreType.DMA((3,)),
            pltpu.SemaphoreType.DMA((2,)),
            pltpu.SemaphoreType.DMA((2,)),
            pltpu.SemaphoreType.DMA((2,)),
        ],
        compiler_params=pltpu.CompilerParams(collective_id=0, has_side_effects=True, vmem_limit_bytes=60 * 1024 * 1024),
        name="gather_grams",
    )(wide, gate_weight, up_weight)


MGROUPS = 8
OFF_WEIGHT = 0.75
RIDGE = 1e-05
OCT = 8


def split_two(value):
    high = value.astype(BF16)
    return high, (value - high.astype(F32)).astype(BF16)


def dot3(left, right, contract=(1, 0)):
    lh, ll = split_two(left)
    rh, rl = split_two(right)
    dims = (((contract[0],), (contract[1],)), ((), ()))
    part = partial(lax.dot_general, dimension_numbers=dims, preferred_element_type=F32)
    return part(lh, rh) + part(lh, rl) + part(ll, rh)


def lane_pick(value, k):
    where = jnp.full(value.shape, k, jnp.int32)
    return jnp.take_along_axis(value, where, axis=1, mode="promise_in_bounds")


def factor(state, systems):
    lanes = lax.broadcasted_iota(jnp.int32, (systems, NB), 1)
    for octet in range(NB // OCT):

        def step(s, carry):
            k = octet * OCT + s
            row = state[k]
            inverse = 1.0 / lane_pick(row, k)
            scaled = (row + (lanes == k).astype(F32)) * inverse
            for t in range(1, OCT):
                i = octet * OCT + t
                other = state[i]
                keep = jnp.where(t > s, 1.0, 0.0)
                state[i] = other - lane_pick(other, k) * (scaled * keep)
            for i in range((octet + 1) * OCT, NB):
                other = state[i]
                state[i] = other - lane_pick(other, k) * scaled
            return carry

        lax.fori_loop(0, OCT, step, 0)


def solve_kernel(group_of, gram_ref, moved_ref, out_ref, sums, state, scales, moved_buf, terms, sem):
    blocks, experts = gram_ref.shape[0], gram_ref.shape[1]
    systems = MGROUPS * blocks
    fetch = pltpu.make_async_copy(moved_ref, moved_buf, sem)
    fetch.start()
    sums[...] = jnp.zeros_like(sums)
    terms[...] = jnp.zeros_like(terms)

    def add_gram(e, carry):
        group = group_of[e]
        for b in range(blocks):
            where = group * blocks + b
            sums[where] = sums[where] + gram_ref[b, e]
        return carry

    lax.fori_loop(0, experts, add_gram, 0)
    rows = lax.broadcasted_iota(jnp.int32, (NB, NB), 0)
    lanes = lax.broadcasted_iota(jnp.int32, (NB, NB), 1)
    same = rows == lanes
    for i in range(systems):
        summed = sums[i]
        diagonal = jnp.where(same, summed + RIDGE, 0.0)
        across = lax.rsqrt(jnp.sum(diagonal, axis=0, keepdims=True))
        down = lax.rsqrt(jnp.sum(diagonal, axis=1, keepdims=True))
        scales[i] = jnp.broadcast_to(across, (8, NB))
        state[:, i, :] = jnp.where(same, diagonal, OFF_WEIGHT * summed) * down * across
    factor(state, systems)
    fetch.wait()

    def add_term(e, carry):
        group = group_of[e]
        for b in range(blocks):
            where = group * blocks + b
            high, low = split_two(gram_ref[b, e])
            moved = moved_buf[e, b]
            terms[where] = terms[where] + (
                jnp.dot(moved, high, preferred_element_type=F32)
                + jnp.dot(moved, low, preferred_element_type=F32)
            )
        return carry

    lax.fori_loop(0, experts, add_term, 0)
    for m in range(MGROUPS):
        for b in range(blocks):
            i = m * blocks + b
            full = state[:, i, :]
            lower = jnp.where(lanes < rows, full, jnp.where(same, 1.0, 0.0))
            inverse = 1.0 / jnp.sum(jnp.where(same, full, 0.0), axis=0, keepdims=True)
            scale = scales[i, 0:1, :]
            half = dot3(terms[i] * scale, lower, (1, 1)) * inverse
            merged = dot3(half, lower, (1, 0)) * scale
            out_ref[m, :, b * NB : (b + 1) * NB] = merged.astype(BF16)


def solve(merge_group, grams, moved):
    blocks, experts = grams.shape[0], grams.shape[1]
    columns = moved.shape[2]
    systems = MGROUPS * blocks
    return pl.pallas_call(
        solve_kernel,
        out_shape=jax.ShapeDtypeStruct((MGROUPS, columns, blocks * NB), BF16),
        grid_spec=pltpu.PrefetchScalarGridSpec(
            num_scalar_prefetch=1,
            grid=(),
            in_specs=[
                pl.BlockSpec(memory_space=pltpu.VMEM),
                pl.BlockSpec(memory_space=pl.ANY),
            ],
            out_specs=pl.BlockSpec(memory_space=pltpu.VMEM),
            scratch_shapes=[
                pltpu.VMEM((systems, NB, NB), F32),
                pltpu.VMEM((NB, systems, NB), F32),
                pltpu.VMEM((systems, 8, NB), F32),
                pltpu.VMEM(moved.shape, BF16),
                pltpu.VMEM((systems, columns, NB), F32),
                pltpu.SemaphoreType.DMA,
            ],
        ),
        name="solve",
    )(merge_group, grams, moved)


def dot_exact(left, right, contract, split_left):
    value, one_hot = (left, right) if split_left else (right, left)
    first = value.astype(BF16)
    rest = value - first.astype(F32)
    second = rest.astype(BF16)
    third = (rest - second.astype(F32)).astype(BF16)
    dims = (((contract[0],), (contract[1],)), ((), ()))
    total = None
    for part in (first, second, third):
        pair = (part, one_hot) if split_left else (one_hot, part)
        term = lax.dot_general(*pair, dims, preferred_element_type=F32)
        total = term if total is None else total + term
    return total


def exchange_kernel(part_ref, selector_ref, gram_ref, inbox, send_sem, recv_sem, relay_send, relay_recv, pair_sem):
    expert = lax.axis_index("expert")
    z = lax.axis_index("group")
    core = lax.rem(expert, 2)
    y = lax.rem(lax.div(expert, 2), YN)
    x = lax.div(expert, 2 * YN)
    partner = (place(x, y, 1 - core), z)

    def device(axis, shift):
        if axis == "x":
            return (place(lax.rem(x + XN + shift, XN), y, core), z)
        return (place(x, lax.rem(y + YN + shift, YN), core), z)

    barrier = pltpu.get_barrier_semaphore()
    neighbours = [device(a, s) for a in "xy" for s in (1, -1)] + [partner]
    for other in neighbours:
        pl.semaphore_signal(barrier, inc=1, device_id=other, device_id_type=MESH)
    pl.semaphore_wait(barrier, len(neighbours))

    swap = pltpu.make_async_remote_copy(
        src_ref=part_ref.at[1 - core],
        dst_ref=inbox,
        send_sem=pair_sem.at[0],
        recv_sem=pair_sem.at[1],
        device_id=partner,
        device_id_type=MESH,
    )
    swap.start()
    blocks = part_ref.shape[1]
    axes = (("x", x), ("y", y))
    swap.wait_recv()
    for b in range(blocks):
        summed = part_ref[core, b] + inbox[b]
        turned = dot_exact(selector_ref[b], summed, (0, 0), False)
        gram_ref[b, x, y, core] = dot_exact(turned, selector_ref[b], (1, 0), True)

    def unit(b, stage, pos, half=None):
        along = axes[b] if stage == 0 else axes[1 - b]
        if stage == 0:
            lead = (b, pos, y, core) if along[0] == "x" else (b, x, pos, core)
            return gram_ref.at[lead + ((pl.ds(half * (NB // 2), NB // 2),) if half is not None else ())]
        other = pl.ds(0, XN) if half is None else pl.ds(half * (XN // 2), XN // 2)
        lead = (b, pos, other, core) if along[0] == "x" else (b, other, pos, core)
        return gram_ref.at[lead]

    started = {}

    def start(b, stage, step):
        axis, pos = axes[b] if stage == 0 else axes[1 - b]
        for way, sign in ((0, 1), (1, -1)):
            half = way if step == 2 else None
            ref = unit(b, stage, lax.rem(pos + XN - sign * (step - 1), XN), half)
            copy = pltpu.make_async_remote_copy(
                src_ref=ref,
                dst_ref=ref,
                send_sem=send_sem.at[b, stage, way, step - 1],
                recv_sem=recv_sem.at[b, stage, way, step - 1],
                device_id=device(axis, sign),
                device_id_type=MESH,
            )
            copy.start()
            started[b, stage, way, step] = copy

    def arrive(b, stage, step):
        for way in (0, 1):
            started[b, stage, way, step].wait_recv()

    relays = []

    def relay(b, shift):
        axis, pos = axes[1 - b]
        ref = unit(b, 1, lax.rem(pos + shift, XN))
        copy = pltpu.make_async_remote_copy(
            src_ref=ref,
            dst_ref=ref,
            send_sem=relay_send.at[b, shift],
            recv_sem=relay_recv.at[b, shift],
            device_id=partner,
            device_id_type=MESH,
        )
        copy.start()
        relays.append(copy)

    for b in range(blocks):
        start(b, 0, 1)
    for b in range(blocks):
        arrive(b, 0, 1)
        start(b, 0, 2)
    for b in range(blocks):
        arrive(b, 0, 2)
        start(b, 1, 1)
    for b in range(blocks):
        relay(b, 0)
    for b in range(blocks):
        arrive(b, 1, 1)
        start(b, 1, 2)
    for b in range(blocks):
        relay(b, 1)
        relay(b, 3)
    for b in range(blocks):
        arrive(b, 1, 2)
        relay(b, 2)
    for copy in relays:
        copy.wait_recv()
        copy.wait_send()
    for copy in started.values():
        copy.wait_send()
    swap.wait_send()


def exchange(partials, selector):
    blocks = partials.shape[1]
    return pl.pallas_call(
        exchange_kernel,
        out_shape=jax.ShapeDtypeStruct((blocks, XN, YN, 2, NB, NB), F32),
        in_specs=[pl.BlockSpec(memory_space=pltpu.VMEM)] * 2,
        out_specs=pl.BlockSpec(memory_space=pltpu.VMEM),
        scratch_shapes=[
            pltpu.VMEM((blocks, NB, NB), F32),
            pltpu.SemaphoreType.DMA((blocks, 2, 2, 2)),
            pltpu.SemaphoreType.DMA((blocks, 2, 2, 2)),
            pltpu.SemaphoreType.DMA((blocks, 4)),
            pltpu.SemaphoreType.DMA((blocks, 4)),
            pltpu.SemaphoreType.DMA((2,)),
        ],
        compiler_params=pltpu.CompilerParams(collective_id=1, has_side_effects=True),
        name="exchange_grams",
    )(partials, selector)


def per_device(tokens, routes, gate_weight, up_weight, down_weight, merge_group, neuron_perm):
    experts = lax.axis_size("expert")
    units = gate_weight.shape[2]
    blocks = units // NB
    width = tokens.shape[1]
    columns = width // experts
    start = lax.axis_index("group") * units + jnp.arange(blocks, dtype=jnp.int32) * NB
    within = neuron_perm.reshape(blocks, NB) - start[:, None]
    selector = (within[:, None, :] == jnp.arange(NB, dtype=jnp.int32)[None, :, None]).astype(BF16)
    moved = jnp.einsum(
        "bid,bin->bdn", down_weight.reshape(blocks, NB, width), selector, preferred_element_type=F32
    ).astype(BF16)
    partials = gather_grams(tokens, routes, gate_weight[0], up_weight[0])
    shaped = moved.reshape(1, blocks, experts, columns, NB)
    spread = lax.all_to_all(shaped, "expert", split_axis=2, concat_axis=0, tiled=True)
    spread = spread.reshape(experts, blocks, columns, NB)
    grams = exchange(partials, selector).reshape(blocks, experts, NB, NB)
    return jnp.swapaxes(solve(merge_group, grams, spread), 1, 2)


def solution(mesh):
    in_specs = (
        P(("expert", "group"), None),
        P(("expert", "group"), None),
        P("expert", None, "group"),
        P("expert", None, "group"),
        P("expert", "group", None),
        P(),
        P("expert", "group"),
    )
    return jax.shard_map(
        per_device, mesh=mesh, in_specs=in_specs, out_specs=P(None, "group", "expert"), check_vma=False
    )
```

```python
from functools import partial

import jax
import jax.numpy as jnp
from jax import lax
from jax.experimental import pallas as pl
from jax.experimental.pallas import tpu as pltpu
from jax.sharding import PartitionSpec as P

NB = 128
F32 = jnp.float32
BF16 = jnp.bfloat16
MESH = pl.DeviceIdType.MESH
XN, YN, ZN = 4, 4, 8
SIZES = {"x": XN, "y": YN, "z": ZN}
ORDERS = ("zyx", "zxy", "yxz")


def place(x, y, core):
    return (x * YN + y) * 2 + core


def offsets(n):
    listed = [0]
    for d in range(1, n // 2):
        listed += [-d, d]
    return listed + [n // 2]


def last_ways(stage, color, n, index):
    if stage == 0:
        return (color % 2,)
    return ((0, 1, 1, 0)[index % 4],)


def transfers():
    found = {}
    for color, order in enumerate(ORDERS):
        for stage, axis in enumerate(order):
            n = SIZES[axis]
            pieces = (None,) if stage == 0 else tuple(offsets(SIZES[order[stage - 1]]))
            for step in range(1, n // 2 + 1):
                for index, piece in enumerate(pieces):
                    ways = (0, 1) if step < n // 2 else last_ways(stage, color, n, index)
                    for way in ways:
                        found[color, stage, way, step, piece] = None
    return found


def arrivals(tasks, color, stage, offset):
    if offset == 0:
        if stage == 0:
            return set()
        below = SIZES[ORDERS[color][stage - 1]]
        return set().union(*(arrivals(tasks, color, stage - 1, d) for d in offsets(below)))
    return {
        t for t in tasks
        if t[0] == color and t[1] == stage and t[3] == abs(offset)
        and (abs(offset) == SIZES[ORDERS[color][stage]] // 2 or t[2] == (0 if offset < 0 else 1))
    }


def schedule(chunks, depth=4.0, shallow=-0.5):
    tasks = transfers()
    needs = {}
    for t in tasks:
        color, stage, way, step, piece = t
        if step > 1:
            needs[t] = {(color, stage, way, step - 1, piece)}
        else:
            needs[t] = arrivals(tasks, color, stage - 1, piece) if stage else set()
    takes = {}
    for color, order in enumerate(ORDERS):
        for d in offsets(SIZES[order[2]]):
            takes["take", color, d] = arrivals(tasks, color, 2, d)
    fill = [("chunk", i) for i in range(chunks)]
    rate, delay = 39e-3 / 0.047, 2.0
    now, busy, landed, waited, plan = 0.0, {}, {}, set(), []

    def flush(need):
        for t in sorted(need - waited, key=lambda t: landed[t]):
            plan.append(("wait", t))
            waited.add(t)

    def urgency(t):
        return (t[1], t[3], 0 if t[4] is None else abs(t[4]), t[0], t[2])

    todo = sorted(tasks, key=urgency)
    while todo or takes:
        ready = [t for t in todo if all(landed.get(d, 1e9) <= now for d in needs[t])]
        queue = []
        for t in ready:
            color, stage, way, step, piece = t
            link = (ORDERS[color][stage], way)
            size = 1 if stage < 2 else SIZES[ORDERS[color][0]]
            urgent = any(u[1] < 2 and (ORDERS[u[0]][u[1]], u[2]) == link for u in todo)
            if stage == 2 and busy.get(link, 0.0) - now > (shallow if urgent else depth):
                continue
            busy[link] = max(busy.get(link, 0.0), now) + size * rate
            landed[t] = busy[link] + delay
            queue.append(t)
        for t in queue:
            flush(needs[t])
            plan.append(("start", t))
            todo.remove(t)
        if queue:
            continue
        open_takes = [k for k in takes if all(landed.get(d, 1e9) <= now for d in takes[k])] if now > 16 else []
        if open_takes:
            key = open_takes[0]
            flush(takes.pop(key))
            plan.append(key)
            now += 1.4 if key[1] < 2 else 1.0
        elif fill and now > 8:
            plan.append(fill.pop(0))
            now += 0.7
        else:
            later = [v for v in landed.values() if v > now] + ([16.001] if now <= 16 else [])
            now = min(later) if later else now + 0.5
    return plan + fill


def gather_kernel(part, width, tok_ref, gate_ref, up_ref, down_ref, perm_ref, merge_ref,
                  out_ref, moved_ref, plan_ref, bufx, bufy, bufz, weights, acc, lhs, down, moved,
                  send_sem, recv_sem, own_sem, wsem, wsend, wrecv, dsem, msem):
    expert = lax.axis_index("expert")
    z = lax.axis_index("group")
    core = lax.rem(expert, 2)
    y = lax.rem(lax.div(expert, 2), YN)
    x = lax.div(expert, 2 * YN)
    here = {"x": x, "y": y, "z": z}
    units = gate_ref.shape[1]
    blocks = units // NB
    experts = moved.shape[0]
    per_chunk = 4
    chunks = experts // per_chunk

    def shifted(axis, shift):
        return lax.rem(here[axis] + SIZES[axis] + shift, SIZES[axis])

    def device(axis, shift):
        at = dict(here)
        at[axis] = shifted(axis, shift)
        return (place(at["x"], at["y"], core), at["z"])

    partner = (place(x, y, 1 - core), z)
    bufs = (bufx, bufy, bufz)
    columns = (0, part, 2 * part)

    load_down = pltpu.make_async_copy(down_ref, down, dsem)
    load_down.start()
    barrier = pltpu.get_barrier_semaphore()
    neighbours = [device(a, s) for a in "xyz" for s in (1, -1)] + [partner]
    for other in neighbours:
        pl.semaphore_signal(barrier, inc=1, device_id=other, device_id_type=MESH)
    pl.semaphore_wait(barrier, len(neighbours))

    numbers = {t: i for i, t in enumerate(transfers())}

    def piece_ref(color, stage, offset, piece):
        order = ORDERS[color]
        buf = bufs[color]
        if stage == 0:
            return buf.at[here[order[2]], here[order[1]], shifted(order[0], offset)]
        if stage == 1:
            return buf.at[here[order[2]], shifted(order[1], offset), shifted(order[0], piece)]
        return buf.at[shifted(order[2], offset), shifted(order[1], piece)]

    started = {}

    def start(task):
        color, stage, way, step, piece = task
        sign = 1 - 2 * way
        dst = piece_ref(color, stage, -sign * (step - 1), piece)
        first = step == 1 and (stage == 0 or (stage == 1 and piece == 0))
        src = tok_ref.at[:, pl.ds(columns[color], part)] if first else dst
        i = numbers[task]
        copy = pltpu.make_async_remote_copy(
            src_ref=src,
            dst_ref=dst,
            send_sem=send_sem.at[i],
            recv_sem=recv_sem.at[i],
            device_id=device(ORDERS[color][stage], sign),
            device_id_type=MESH,
        )
        copy.start()
        started[task] = copy

    own = []
    for color in range(3):
        copy = pltpu.make_async_copy(
            tok_ref.at[:, pl.ds(columns[color], part)], piece_ref(color, 0, 0, None), own_sem.at[color]
        )
        copy.start()
        own.append(copy)
    moves = []

    def move_weights():
        for j, ref in enumerate((gate_ref, up_ref)):
            local = pltpu.make_async_copy(ref, weights.at[core * 2 + j], wsem.at[j])
            local.start()
            remote = pltpu.make_async_remote_copy(
                src_ref=ref,
                dst_ref=weights.at[core * 2 + j],
                send_sem=wsend.at[j],
                recv_sem=wrecv.at[j],
                device_id=partner,
                device_id_type=MESH,
            )
            remote.start()
            moves.append((local, remote))

    def multiply(rows, depth, first_row, color, plane):
        def per_column(n, carry):
            w = weights[n, pl.ds(first_row, depth), :]
            value = jnp.dot(lhs[0:rows, 0:depth], w, preferred_element_type=F32)
            if color == 0:
                acc[n, plane] += value.reshape(YN, ZN, 8, units)
            elif color == 1:
                acc[n, :, plane] += value.reshape(XN, ZN, 8, units)
            else:
                acc[n, :, :, plane] += value.reshape(XN, YN, 8, units)
            return carry

        lax.fori_loop(0, 4, per_column, 0)

    def take(color, offset):
        plane = shifted(ORDERS[color][2], offset)
        depth = part if color < 2 else width - 2 * part
        rows = 256 if color < 2 else 128
        value = bufs[color][plane, :, :, :, 0:depth].astype(F32)
        lhs[0:rows, 0:depth] = value.reshape(rows, depth).astype(BF16)
        multiply(rows, depth, columns[color], color, plane)

    unit_rows = lax.broadcasted_iota(jnp.int32, (NB, NB), 0)
    span = per_chunk * (width // experts)
    writes = []

    def chunk(i):
        for b in range(blocks):
            within = perm_ref[0:1, b * NB : (b + 1) * NB] - (z * units + b * NB)
            selector = (unit_rows == within).astype(F32).astype(BF16)
            piece = down[b * NB : (b + 1) * NB, i * span : (i + 1) * span]
            turned = lax.dot_general(piece, selector, (((0,), (0,)), ((), ())), preferred_element_type=F32)
            moved[i * per_chunk : (i + 1) * per_chunk, b] = turned.astype(BF16).reshape(per_chunk, span // per_chunk, NB)
        copy = pltpu.make_async_copy(
            moved.at[pl.ds(i * per_chunk, per_chunk)], moved_ref.at[pl.ds(i * per_chunk, per_chunk)], msem.at[i]
        )
        copy.start()
        writes.append(copy)

    order = schedule(chunks)
    begun = False
    settled = False
    for action, *rest in order:
        if action == "start":
            if not settled and rest[0][1] > 0:
                for copy in own:
                    copy.wait()
                settled = True
            start(rest[0])
        elif not begun:
            move_weights()
            acc[...] = jnp.zeros_like(acc)
            begun = True
        if action == "wait":
            started[rest[0]].wait_recv()
        elif action == "chunk":
            if rest[0] == 0:
                load_down.wait()
            chunk(rest[0])
        elif action == "take":
            if moves[0] is not None:
                for local, remote in moves:
                    local.wait()
                    remote.wait_recv()
                sent = [remote for _, remote in moves]
                moves[0] = None
            take(*rest)

    out_ref[...] = jnp.zeros_like(out_ref)
    spare = width - 2 * part

    def finish(i, carry):
        px, p = lax.div(i, 2), lax.rem(i, 2)
        named = (place(x, y, 0) + p).astype(F32)
        gate = acc[2 * p, px].reshape(256, units)
        up = acc[2 * p + 1, px].reshape(256, units)
        listed = jnp.concatenate(
            [bufz[:, px, py, :, spare : spare + NB].astype(F32).reshape(ZN * 8, NB) for py in range(YN)], axis=0
        )
        chosen = jnp.max(jnp.where(listed == named, 1.0, 0.0), axis=1, keepdims=True)
        value = gate / (1.0 + jnp.exp(-gate)) * up
        hidden = jnp.where(chosen > 0.5, value, 0.0).astype(BF16)
        for b in range(blocks):
            piece = hidden[:, b * NB : (b + 1) * NB]
            out_ref[p, b] += lax.dot_general(piece, piece, (((0,), (0,)), ((), ())), preferred_element_type=F32)
        return carry

    lax.fori_loop(0, 2 * XN, finish, 0)

    count = merge_ref.shape[1]
    ids = lax.broadcasted_iota(jnp.int32, (count, count), 0).astype(F32)
    lanes = lax.broadcasted_iota(jnp.int32, (count, count), 1).astype(F32)
    across = jnp.broadcast_to(merge_ref[0:1, :].astype(F32), (count, count))
    down_way = jnp.sum(jnp.where(ids == lanes, across, 0.0), axis=1, keepdims=True)
    before = (across < down_way) | ((across == down_way) & (lanes < ids))
    rank = jnp.sum(jnp.where(before, 1.0, 0.0), axis=1, keepdims=True)
    here_rank = rank == lanes
    after_rank = rank == lanes - 1.0
    listed = jnp.sum(jnp.where(here_rank, ids, 0.0), axis=0, keepdims=True)
    own_group = jnp.sum(jnp.where(here_rank, down_way, 0.0), axis=0, keepdims=True)
    last_group = jnp.sum(jnp.where(after_rank, down_way + 1.0, 0.0), axis=0, keepdims=True) - 1.0
    keep = jnp.where(own_group == last_group, 1.0, 0.0)
    ends = jnp.sum(jnp.where(down_way <= lanes, 1.0, 0.0), axis=0, keepdims=True) - 1.0
    plan_ref[...] = jnp.concatenate([listed, keep, ends], axis=0).astype(jnp.int32)

    for copy in started.values():
        copy.wait_send()
    for remote in sent:
        remote.wait_send()
    for copy in writes:
        copy.wait()


def gather_grams(tokens, routes, gate_weight, up_weight, down_weight, neuron_perm, merge_group):
    rows, width = tokens.shape
    units = gate_weight.shape[1]
    blocks = units // NB
    experts = merge_group.shape[0]
    listed = jnp.pad(routes.astype(BF16), ((0, 0), (0, NB - routes.shape[1])), constant_values=-1)
    wide = jnp.concatenate([tokens, listed], axis=1)
    part = (width + NB) // 3
    number = len(transfers())
    moved_shape = (experts, blocks, width // experts, NB)
    return pl.pallas_call(
        partial(gather_kernel, part, width),
        out_shape=(
            jax.ShapeDtypeStruct((2, blocks, NB, NB), F32),
            jax.ShapeDtypeStruct(moved_shape, BF16),
            jax.ShapeDtypeStruct((3, experts), jnp.int32),
        ),
        in_specs=[pl.BlockSpec(memory_space=pl.ANY)] * 4 + [pl.BlockSpec(memory_space=pltpu.VMEM)] * 2,
        out_specs=(
            pl.BlockSpec(memory_space=pltpu.VMEM),
            pl.BlockSpec(memory_space=pl.ANY),
            pl.BlockSpec(memory_space=pltpu.VMEM),
        ),
        scratch_shapes=[
            pltpu.VMEM((XN, YN, ZN, 8, part), BF16),
            pltpu.VMEM((YN, XN, ZN, 8, part), BF16),
            pltpu.VMEM((ZN, XN, YN, 8, part), BF16),
            pltpu.VMEM((4, width, units), BF16),
            pltpu.VMEM((4, XN, YN, ZN, 8, units), F32),
            pltpu.VMEM((256, part), BF16),
            pltpu.VMEM((units, width), BF16),
            pltpu.VMEM(moved_shape, BF16),
            pltpu.SemaphoreType.DMA((number,)),
            pltpu.SemaphoreType.DMA((number,)),
            pltpu.SemaphoreType.DMA((3,)),
            pltpu.SemaphoreType.DMA((2,)),
            pltpu.SemaphoreType.DMA((2,)),
            pltpu.SemaphoreType.DMA((2,)),
            pltpu.SemaphoreType.DMA,
            pltpu.SemaphoreType.DMA((8,)),
        ],
        compiler_params=pltpu.CompilerParams(collective_id=0, has_side_effects=True, vmem_limit_bytes=60 * 1024 * 1024),
        name="gather_grams",
    )(wide, gate_weight, up_weight, down_weight, neuron_perm, merge_group[None, :])


MGROUPS = 8
OFF_WEIGHT = 0.75
RIDGE = 1e-05
LOW = 16
BATCH = 4
HIGH = NB // LOW


def split_two(value):
    high = value.astype(BF16)
    return high, (value - high.astype(F32)).astype(BF16)


def dot3(left, right, contract):
    lh, ll = split_two(left)
    rh, rl = split_two(right)
    dims = (((1,), (contract,)), ((), ()))
    part = partial(lax.dot_general, dimension_numbers=dims, preferred_element_type=F32)
    return part(lh, rh) + part(lh, rl) + part(ll, rh)


def dot_exact(value, one_hot, value_left, contract):
    first = value.astype(BF16)
    rest = value - first.astype(F32)
    second = rest.astype(BF16)
    third = (rest - second.astype(F32)).astype(BF16)
    dims = (((contract,), (0,)), ((), ())) if value_left else (((0,), (contract,)), ((), ()))
    total = None
    for part in (first, second, third):
        pair = (part, one_hot) if value_left else (one_hot, part)
        term = lax.dot_general(*pair, dims, preferred_element_type=F32)
        total = term if total is None else total + term
    return total


def regroup(state, lanes):
    for bit in (1, 2, 4, 8):
        low = (lanes & bit) == 0
        for m in range(LOW):
            if m & bit:
                continue
            first, second = state[m], state[m | bit]
            state[m] = jnp.where(low, first, pltpu.roll(second, bit, 1))
            state[m | bit] = jnp.where(low, pltpu.roll(first, NB - bit, 1), second)


def eliminate(state, rows, lanes):
    def prepare(q, g):
        k = g * LOW + q
        pick = g * LOW + (lanes & (LOW - 1))
        row = jnp.take_along_axis(state[q], pick, axis=1, mode="promise_in_bounds")
        at_pivot = jnp.broadcast_to(state[q, pl.ds(k, 1), :], (8, NB))
        pivot = jnp.take_along_axis(at_pivot, pick[0:8], axis=1, mode="promise_in_bounds")
        inverse = (1.0 / pivot)[0:1]
        return (row + (rows == k).astype(F32)) * inverse

    for q in range(LOW):

        def step(g, scaled):
            k = g * LOW + q
            column = state[q, pl.ds(k, 1), :]
            column = jnp.where(lanes[0:1] >= (g + 1) * LOW, column, 0.0)
            state[q] = state[q] - column * scaled
            following = prepare(q, jnp.minimum(g + 1, HIGH - 1))
            for later in range(q + 1, LOW):
                state[later] = state[later] - state[later, pl.ds(k, 1), :] * scaled
            return following

        lax.fori_loop(0, HIGH, step, prepare(q, 0))


def solve_kernel(part_ref, perm_ref, plan_ref, moved_ref, out_ref, gram_ref, inbox, spread, runs, state, terms, scales,
                 send_sem, recv_sem, relay_send, relay_recv, pair_sem, all_send, all_recv, own_sem):
    expert = lax.axis_index("expert")
    z = lax.axis_index("group")
    core = lax.rem(expert, 2)
    y = lax.rem(lax.div(expert, 2), YN)
    x = lax.div(expert, 2 * YN)
    partner = (place(x, y, 1 - core), z)
    blocks = part_ref.shape[1]
    units = blocks * NB
    experts = spread.shape[0]
    rows = lax.broadcasted_iota(jnp.int32, (NB, NB), 0)
    lanes = lax.broadcasted_iota(jnp.int32, (NB, NB), 1)
    same = rows == lanes

    def device(axis, shift):
        if axis == "x":
            return (place(lax.rem(x + XN + shift, XN), y, core), z)
        return (place(x, lax.rem(y + YN + shift, YN), core), z)

    others = [(dx, dy, dc) for dx in range(XN) for dy in range(YN) for dc in range(2) if dx or dy or dc]

    def other(dx, dy, dc):
        return place(lax.rem(x + dx, XN), lax.rem(y + dy, YN), lax.rem(core + dc, 2))

    barrier = pltpu.get_barrier_semaphore()
    for shift in others:
        pl.semaphore_signal(barrier, inc=1, device_id=(other(*shift), z), device_id_type=MESH)
    pl.semaphore_wait(barrier, len(others))

    swap = pltpu.make_async_remote_copy(
        src_ref=part_ref.at[1 - core],
        dst_ref=inbox,
        send_sem=pair_sem.at[0],
        recv_sem=pair_sem.at[1],
        device_id=partner,
        device_id_type=MESH,
    )
    swap.start()
    axes = (("x", x), ("y", y))
    swap.wait_recv()
    for b in range(blocks):
        selector = (rows == perm_ref[0:1, b * NB : (b + 1) * NB] - (z * units + b * NB)).astype(F32).astype(BF16)
        summed = part_ref[core, b] + inbox[b]
        turned = dot_exact(summed, selector, False, 0)
        gram_ref[b, x, y, core] = dot_exact(turned, selector, True, 1)

    def unit(b, stage, pos, half=None):
        along = axes[b] if stage == 0 else axes[1 - b]
        if stage == 0:
            lead = (b, pos, y, core) if along[0] == "x" else (b, x, pos, core)
            return gram_ref.at[lead + ((pl.ds(half * (NB // 2), NB // 2),) if half is not None else ())]
        ring = pl.ds(0, XN) if half is None else pl.ds(half * (XN // 2), XN // 2)
        lead = (b, pos, ring, core) if along[0] == "x" else (b, ring, pos, core)
        return gram_ref.at[lead]

    started = {}

    def start(b, stage, step):
        axis, pos = axes[b] if stage == 0 else axes[1 - b]
        for way, sign in ((0, 1), (1, -1)):
            half = way if step == 2 else None
            ref = unit(b, stage, lax.rem(pos + XN - sign * (step - 1), XN), half)
            copy = pltpu.make_async_remote_copy(
                src_ref=ref,
                dst_ref=ref,
                send_sem=send_sem.at[b, stage, way, step - 1],
                recv_sem=recv_sem.at[b, stage, way, step - 1],
                device_id=device(axis, sign),
                device_id_type=MESH,
            )
            copy.start()
            started[b, stage, way, step] = copy

    def arrive(b, stage, step):
        for way in (0, 1):
            started[b, stage, way, step].wait_recv()

    relays = []

    def relay(b, shift):
        axis, pos = axes[1 - b]
        ref = unit(b, 1, lax.rem(pos + shift, XN))
        copy = pltpu.make_async_remote_copy(
            src_ref=ref,
            dst_ref=ref,
            send_sem=relay_send.at[b, shift],
            recv_sem=relay_recv.at[b, shift],
            device_id=partner,
            device_id_type=MESH,
        )
        copy.start()
        relays.append(copy)

    spreads = []

    def spread_some(which):
        for i in which:
            to = other(*others[i])
            copy = pltpu.make_async_remote_copy(
                src_ref=moved_ref.at[to],
                dst_ref=spread.at[expert],
                send_sem=all_send.at[i],
                recv_sem=all_recv.at[i],
                device_id=(to, z),
                device_id_type=MESH,
            )
            copy.start()
            spreads.append(copy)

    for b in range(blocks):
        start(b, 0, 1)
    for b in range(blocks):
        arrive(b, 0, 1)
        start(b, 0, 2)
    for b in range(blocks):
        arrive(b, 0, 2)
        start(b, 1, 1)
    for b in range(blocks):
        relay(b, 0)
    for b in range(blocks):
        arrive(b, 1, 1)
        start(b, 1, 2)
    for b in range(blocks):
        relay(b, 1)
        relay(b, 3)
    spread_some(range(len(others)))
    own = pltpu.make_async_copy(moved_ref.at[expert], spread.at[expert], own_sem)
    own.start()
    for b in range(blocks):
        arrive(b, 1, 2)
        relay(b, 2)
    for copy in relays:
        copy.wait_recv()

    def gram_of(b, e):
        return gram_ref[b, lax.div(e, 2 * YN), lax.rem(lax.div(e, 2), YN), lax.rem(e, 2)]

    for b in range(blocks):

        def add_grams(i, run):
            for d in range(BATCH):
                j = i * BATCH + d
                run = run * plan_ref[1, j].astype(F32) + gram_of(b, plan_ref[0, j])
                runs[j, 0:NB, :] = run
            return run

        lax.fori_loop(0, experts // BATCH, add_grams, jnp.zeros((NB, NB), F32))
        for m in range(MGROUPS):
            summed = runs[plan_ref[2, m], 0:NB, :]
            diagonal = jnp.where(same, summed + RIDGE, 0.0)
            across = lax.rsqrt(jnp.sum(diagonal, axis=0, keepdims=True))
            down = lax.rsqrt(jnp.sum(diagonal, axis=1, keepdims=True))
            i = m * blocks + b
            scales[i] = jnp.broadcast_to(across, (8, NB))
            state[i] = jnp.where(same, diagonal, OFF_WEIGHT * summed) * down * across

    regroup(state, lanes)
    eliminate(state, rows, lanes)
    regroup(state, lanes)

    own.wait()
    for copy in spreads:
        copy.wait_recv()

    for b in range(blocks):

        def add_terms(i, run):
            made = []
            for d in range(BATCH):
                e = plan_ref[0, i * BATCH + d]
                high, low = split_two(gram_of(b, e))
                moved = spread[e, b]
                made.append(
                    jnp.dot(
                        jnp.concatenate([moved, moved], axis=1),
                        jnp.concatenate([high, low], axis=0),
                        preferred_element_type=F32,
                    )
                )
            for d in range(BATCH):
                run = run * plan_ref[1, i * BATCH + d].astype(F32) + made[d]
                runs[i * BATCH + d] = run
            return run

        lax.fori_loop(0, experts // BATCH, add_terms, jnp.zeros(runs.shape[1:], F32))
        for m in range(MGROUPS):
            terms[m * blocks + b] = runs[plan_ref[2, m]]

    turn_rows = (rows & (LOW - 1)) * HIGH + lax.shift_right_logical(rows, 4)
    turn_lanes = (lanes & (LOW - 1)) * HIGH + lax.shift_right_logical(lanes, 4)
    earlier = turn_rows < turn_lanes
    for m in range(MGROUPS):
        for b in range(blocks):
            i = m * blocks + b
            full = state[i]
            lower = jnp.where(earlier, full, jnp.where(same, 1.0, 0.0))
            inverse = 1.0 / jnp.sum(jnp.where(same, full, 0.0), axis=0, keepdims=True)
            scale = scales[i, 0:1, :]
            half = dot3(terms[i] * scale, lower, 0) * inverse
            merged = dot3(half, lower, 1) * scale
            out_ref[m, :, b * NB : (b + 1) * NB] = merged.astype(BF16)

    for copy in relays + spreads + list(started.values()):
        copy.wait_send()
    swap.wait_send()


def solve(partials, neuron_perm, plan, moved):
    experts, blocks, columns, _ = moved.shape
    systems = MGROUPS * blocks
    return pl.pallas_call(
        solve_kernel,
        out_shape=jax.ShapeDtypeStruct((MGROUPS, columns, blocks * NB), BF16),
        in_specs=[
            pl.BlockSpec(memory_space=pltpu.VMEM),
            pl.BlockSpec(memory_space=pltpu.VMEM),
            pl.BlockSpec(memory_space=pltpu.SMEM),
            pl.BlockSpec(memory_space=pl.ANY),
        ],
        out_specs=pl.BlockSpec(memory_space=pltpu.VMEM),
        scratch_shapes=[
            pltpu.VMEM((blocks, XN, YN, 2, NB, NB), F32),
            pltpu.VMEM((blocks, NB, NB), F32),
            pltpu.VMEM(moved.shape, BF16),
            pltpu.VMEM((experts, columns, NB), F32),
            pltpu.VMEM((systems, NB, NB), F32),
            pltpu.VMEM((systems, columns, NB), F32),
            pltpu.VMEM((systems, 8, NB), F32),
            pltpu.SemaphoreType.DMA((blocks, 2, 2, 2)),
            pltpu.SemaphoreType.DMA((blocks, 2, 2, 2)),
            pltpu.SemaphoreType.DMA((blocks, 4)),
            pltpu.SemaphoreType.DMA((blocks, 4)),
            pltpu.SemaphoreType.DMA((2,)),
            pltpu.SemaphoreType.DMA((experts - 1,)),
            pltpu.SemaphoreType.DMA((experts - 1,)),
            pltpu.SemaphoreType.DMA,
        ],
        compiler_params=pltpu.CompilerParams(collective_id=1, has_side_effects=True, vmem_limit_bytes=50 * 1024 * 1024),
        name="solve",
    )(partials, neuron_perm, plan, moved)


def per_device(tokens, routes, gate_weight, up_weight, down_weight, merge_group, neuron_perm):
    partials, moved, plan = gather_grams(
        tokens, routes, gate_weight[0], up_weight[0], down_weight[0], neuron_perm, merge_group
    )
    return jnp.swapaxes(solve(partials, neuron_perm, plan, moved), 1, 2)


def solution(mesh):
    in_specs = (
        P(("expert", "group"), None),
        P(("expert", "group"), None),
        P("expert", None, "group"),
        P("expert", None, "group"),
        P("expert", "group", None),
        P(),
        P("expert", "group"),
    )
    return jax.shard_map(
        per_device, mesh=mesh, in_specs=in_specs, out_specs=P(None, "group", "expert"), check_vma=False
    )
```

```python
from functools import partial

import jax
import jax.numpy as jnp
from jax import lax
from jax.experimental import pallas as pl
from jax.experimental.pallas import tpu as pltpu
from jax.sharding import PartitionSpec as P

NB = 128
F32 = jnp.float32
BF16 = jnp.bfloat16
MESH = pl.DeviceIdType.MESH
XN, YN, ZN = 4, 4, 8
SIZES = {"x": XN, "y": YN, "z": ZN}
ORDERS = ("zyx", "zxy", "yxz")


def place(x, y, core):
    return (x * YN + y) * 2 + core


def offsets(n):
    listed = [0]
    for d in range(1, n // 2):
        listed += [-d, d]
    return listed + [n // 2]


def last_ways(stage, color, n, index):
    if stage == 0:
        return (color % 2,)
    return ((0, 1, 1, 0)[index % 4],)


def transfers():
    found = {}
    for color, order in enumerate(ORDERS):
        for stage, axis in enumerate(order):
            n = SIZES[axis]
            pieces = (None,) if stage == 0 else tuple(offsets(SIZES[order[stage - 1]]))
            for step in range(1, n // 2 + 1):
                for index, piece in enumerate(pieces):
                    ways = (0, 1) if step < n // 2 else last_ways(stage, color, n, index)
                    for way in ways:
                        found[color, stage, way, step, piece] = None
    return found


def arrivals(tasks, color, stage, offset):
    if offset == 0:
        if stage == 0:
            return set()
        below = SIZES[ORDERS[color][stage - 1]]
        return set().union(*(arrivals(tasks, color, stage - 1, d) for d in offsets(below)))
    return {
        t for t in tasks
        if t[0] == color and t[1] == stage and t[3] == abs(offset)
        and (abs(offset) == SIZES[ORDERS[color][stage]] // 2 or t[2] == (0 if offset < 0 else 1))
    }


def schedule(chunks, depth=4.0, shallow=-0.5):
    tasks = transfers()
    needs = {}
    for t in tasks:
        color, stage, way, step, piece = t
        if step > 1:
            needs[t] = {(color, stage, way, step - 1, piece)}
        else:
            needs[t] = arrivals(tasks, color, stage - 1, piece) if stage else set()
    takes = {}
    for color, order in enumerate(ORDERS):
        for d in offsets(SIZES[order[2]]):
            takes["take", color, d] = arrivals(tasks, color, 2, d)
    fill = [("chunk", i) for i in range(chunks)]
    rate, delay = 39e-3 / 0.047, 2.0
    now, busy, landed, waited, plan = 0.0, {}, {}, set(), []

    def flush(need):
        for t in sorted(need - waited, key=lambda t: landed[t]):
            plan.append(("wait", t))
            waited.add(t)

    def urgency(t):
        return (t[1], t[3], 0 if t[4] is None else abs(t[4]), t[0], t[2])

    todo = sorted(tasks, key=urgency)
    while todo or takes:
        ready = [t for t in todo if all(landed.get(d, 1e9) <= now for d in needs[t])]
        queue = []
        for t in ready:
            color, stage, way, step, piece = t
            link = (ORDERS[color][stage], way)
            size = 1 if stage < 2 else SIZES[ORDERS[color][0]]
            urgent = any(u[1] < 2 and (ORDERS[u[0]][u[1]], u[2]) == link for u in todo)
            if stage == 2 and busy.get(link, 0.0) - now > (shallow if urgent else depth):
                continue
            busy[link] = max(busy.get(link, 0.0), now) + size * rate
            landed[t] = busy[link] + delay
            queue.append(t)
        for t in queue:
            flush(needs[t])
            plan.append(("start", t))
            todo.remove(t)
        if queue:
            continue
        open_takes = [k for k in takes if all(landed.get(d, 1e9) <= now for d in takes[k])] if now > 16 else []
        if open_takes:
            key = open_takes[0]
            flush(takes.pop(key))
            plan.append(key)
            now += 1.4 if key[1] < 2 else 1.0
        elif fill and now > 8:
            plan.append(fill.pop(0))
            now += 0.7
        else:
            later = [v for v in landed.values() if v > now] + ([16.001] if now <= 16 else [])
            now = min(later) if later else now + 0.5
    return plan + fill


MGROUPS = 8
OFF_WEIGHT = 0.75
RIDGE = 1e-05
LOW = 16
BATCH = 4
EARLY = 16
HIGH = NB // LOW


def split_two(value):
    high = value.astype(BF16)
    return high, (value - high.astype(F32)).astype(BF16)


def dot3(left, right, contract):
    lh, ll = split_two(left)
    rh, rl = split_two(right)
    dims = (((1,), (contract,)), ((), ()))
    part = partial(lax.dot_general, dimension_numbers=dims, preferred_element_type=F32)
    return part(lh, rh) + part(lh, rl) + part(ll, rh)


def dot_exact(value, one_hot, value_left, contract):
    first = value.astype(BF16)
    rest = value - first.astype(F32)
    second = rest.astype(BF16)
    third = (rest - second.astype(F32)).astype(BF16)
    dims = (((contract,), (0,)), ((), ())) if value_left else (((0,), (contract,)), ((), ()))
    total = None
    for part in (first, second, third):
        pair = (part, one_hot) if value_left else (one_hot, part)
        term = lax.dot_general(*pair, dims, preferred_element_type=F32)
        total = term if total is None else total + term
    return total


def regroup(state, lanes):
    for bit in (1, 2, 4, 8):
        low = (lanes & bit) == 0
        for m in range(LOW):
            if m & bit:
                continue
            first, second = state[m], state[m | bit]
            state[m] = jnp.where(low, first, pltpu.roll(second, bit, 1))
            state[m | bit] = jnp.where(low, pltpu.roll(first, NB - bit, 1), second)


def eliminate(state, rows, lanes):
    def prepare(q, g):
        k = g * LOW + q
        pick = g * LOW + (lanes & (LOW - 1))
        row = jnp.take_along_axis(state[q], pick, axis=1, mode="promise_in_bounds")
        at_pivot = jnp.broadcast_to(state[q, pl.ds(k, 1), :], (8, NB))
        pivot = jnp.take_along_axis(at_pivot, pick[0:8], axis=1, mode="promise_in_bounds")
        inverse = (1.0 / pivot)[0:1]
        return (row + (rows == k).astype(F32)) * inverse

    for q in range(LOW):

        def step(g, scaled):
            k = g * LOW + q
            column = state[q, pl.ds(k, 1), :]
            column = jnp.where(lanes[0:1] >= (g + 1) * LOW, column, 0.0)
            state[q] = state[q] - column * scaled
            following = prepare(q, jnp.minimum(g + 1, HIGH - 1))
            for later in range(q + 1, LOW):
                state[later] = state[later] - state[later, pl.ds(k, 1), :] * scaled
            return following

        lax.fori_loop(0, HIGH, step, prepare(q, 0))


def merge_kernel(part, width, tok_ref, gate_ref, up_ref, down_ref, perm_ref, merge_ref, out_ref,
                 bufx, bufy, bufz, weights, acc, lhs, down, moved, part_ref, plan_rows, plan_ref,
                 gram_ref, inbox, spread, runs, state, terms, scales,
                 send_sem, recv_sem, own_sem, wsem, wsend, wrecv, dsem, plan_sem,
                 ring_send, ring_recv, relay_send, relay_recv, pair_sem, all_send, all_recv, keep_sem):
    expert = lax.axis_index("expert")
    z = lax.axis_index("group")
    core = lax.rem(expert, 2)
    y = lax.rem(lax.div(expert, 2), YN)
    x = lax.div(expert, 2 * YN)
    here = {"x": x, "y": y, "z": z}
    units = gate_ref.shape[1]
    blocks = units // NB
    experts = moved.shape[0]
    per_chunk = 4
    chunks = experts // per_chunk

    def shifted(axis, shift):
        return lax.rem(here[axis] + SIZES[axis] + shift, SIZES[axis])

    def device(axis, shift):
        at = dict(here)
        at[axis] = shifted(axis, shift)
        return (place(at["x"], at["y"], core), at["z"])

    partner = (place(x, y, 1 - core), z)
    bufs = (bufx, bufy, bufz)
    columns = (0, part, 2 * part)

    load_down = pltpu.make_async_copy(down_ref, down, dsem)
    load_down.start()
    barrier = pltpu.get_barrier_semaphore()
    others = [(dx, dy, dc) for dx in range(XN) for dy in range(YN) for dc in range(2) if dx or dy or dc]
    others = [others[(i * 13) % len(others)] for i in range(len(others))]

    def other(dx, dy, dc):
        return place(lax.rem(x + dx, XN), lax.rem(y + dy, YN), lax.rem(core + dc, 2))

    neighbours = [device("z", s) for s in (1, -1)] + [(other(*shift), z) for shift in others]
    for to in neighbours:
        pl.semaphore_signal(barrier, inc=1, device_id=to, device_id_type=MESH)
    pl.semaphore_wait(barrier, len(neighbours))

    numbers = {t: i for i, t in enumerate(transfers())}

    def piece_ref(color, stage, offset, piece):
        order = ORDERS[color]
        buf = bufs[color]
        if stage == 0:
            return buf.at[here[order[2]], here[order[1]], shifted(order[0], offset)]
        if stage == 1:
            return buf.at[here[order[2]], shifted(order[1], offset), shifted(order[0], piece)]
        return buf.at[shifted(order[2], offset), shifted(order[1], piece)]

    started = {}

    def start(task):
        color, stage, way, step, piece = task
        sign = 1 - 2 * way
        dst = piece_ref(color, stage, -sign * (step - 1), piece)
        first = step == 1 and (stage == 0 or (stage == 1 and piece == 0))
        src = tok_ref.at[:, pl.ds(columns[color], part)] if first else dst
        i = numbers[task]
        copy = pltpu.make_async_remote_copy(
            src_ref=src,
            dst_ref=dst,
            send_sem=send_sem.at[i],
            recv_sem=recv_sem.at[i],
            device_id=device(ORDERS[color][stage], sign),
            device_id_type=MESH,
        )
        copy.start()
        started[task] = copy

    own = []
    for color in range(3):
        copy = pltpu.make_async_copy(
            tok_ref.at[:, pl.ds(columns[color], part)], piece_ref(color, 0, 0, None), own_sem.at[color]
        )
        copy.start()
        own.append(copy)
    moves = []

    def move_weights():
        for j, ref in enumerate((gate_ref, up_ref)):
            local = pltpu.make_async_copy(ref, weights.at[core * 2 + j], wsem.at[j])
            local.start()
            remote = pltpu.make_async_remote_copy(
                src_ref=ref,
                dst_ref=weights.at[core * 2 + j],
                send_sem=wsend.at[j],
                recv_sem=wrecv.at[j],
                device_id=partner,
                device_id_type=MESH,
            )
            remote.start()
            moves.append((local, remote))

    def multiply(rows, depth, first_row, color, plane):
        def per_column(n, carry):
            w = weights[n, pl.ds(first_row, depth), :]
            value = jnp.dot(lhs[0:rows, 0:depth], w, preferred_element_type=F32)
            if color == 0:
                acc[n, plane] += value.reshape(YN, ZN, 8, units)
            elif color == 1:
                acc[n, :, plane] += value.reshape(XN, ZN, 8, units)
            else:
                acc[n, :, :, plane] += value.reshape(XN, YN, 8, units)
            return carry

        lax.fori_loop(0, 4, per_column, 0)

    def take(color, offset):
        plane = shifted(ORDERS[color][2], offset)
        depth = part if color < 2 else width - 2 * part
        rows = 256 if color < 2 else 128
        value = bufs[color][plane, :, :, :, 0:depth].astype(F32)
        lhs[0:rows, 0:depth] = value.reshape(rows, depth).astype(BF16)
        multiply(rows, depth, columns[color], color, plane)

    unit_rows = lax.broadcasted_iota(jnp.int32, (NB, NB), 0)
    span = per_chunk * (width // experts)

    def chunk(i):
        for b in range(blocks):
            within = perm_ref[0:1, b * NB : (b + 1) * NB] - (z * units + b * NB)
            selector = (unit_rows == within).astype(F32).astype(BF16)
            piece = down[b * NB : (b + 1) * NB, i * span : (i + 1) * span]
            turned = lax.dot_general(piece, selector, (((0,), (0,)), ((), ())), preferred_element_type=F32)
            moved[i * per_chunk : (i + 1) * per_chunk, b] = turned.astype(BF16).reshape(per_chunk, span // per_chunk, NB)

    spreads = []

    def spread_some(which):
        for i in which:
            to = other(*others[i])
            copy = pltpu.make_async_remote_copy(
                src_ref=moved.at[to],
                dst_ref=spread.at[expert],
                send_sem=all_send.at[i],
                recv_sem=all_recv.at[i],
                device_id=(to, z),
                device_id_type=MESH,
            )
            copy.start()
            spreads.append(copy)

    order = schedule(chunks)
    starts_left = len(numbers)
    begun = False
    settled = False
    for action, *rest in order:
        if action == "start":
            if not settled and rest[0][1] > 0:
                for copy in own:
                    copy.wait()
                settled = True
            start(rest[0])
            starts_left -= 1
            if starts_left == 0:
                spread_some(range(EARLY))
        elif not begun:
            move_weights()
            acc[...] = jnp.zeros_like(acc)
            begun = True
        if action == "wait":
            started[rest[0]].wait_recv()
        elif action == "chunk":
            if rest[0] == 0:
                load_down.wait()
            chunk(rest[0])
        elif action == "take":
            if moves[0] is not None:
                for local, remote in moves:
                    local.wait()
                    remote.wait_recv()
                sent = [remote for _, remote in moves]
                moves[0] = None
            take(*rest)

    part_ref[...] = jnp.zeros_like(part_ref)
    spare = width - 2 * part

    def finish(i, carry):
        px, p = lax.rem(i, XN), lax.rem(1 - core + lax.div(i, XN), 2)
        named = (place(x, y, 0) + p).astype(F32)
        gate = acc[2 * p, px].reshape(256, units)
        up = acc[2 * p + 1, px].reshape(256, units)
        listed = jnp.concatenate(
            [bufz[:, px, py, :, spare : spare + NB].astype(F32).reshape(ZN * 8, NB) for py in range(YN)], axis=0
        )
        chosen = jnp.max(jnp.where(listed == named, 1.0, 0.0), axis=1, keepdims=True)
        value = gate / (1.0 + jnp.exp(-gate)) * up
        hidden = jnp.where(chosen > 0.5, value, 0.0).astype(BF16)
        for b in range(blocks):
            piece = hidden[:, b * NB : (b + 1) * NB]
            part_ref[p, b] += lax.dot_general(piece, piece, (((0,), (0,)), ((), ())), preferred_element_type=F32)
        return carry

    lax.fori_loop(0, 2 * XN, finish, 0)
    swap = pltpu.make_async_remote_copy(
        src_ref=part_ref.at[1 - core],
        dst_ref=inbox,
        send_sem=pair_sem.at[0],
        recv_sem=pair_sem.at[1],
        device_id=partner,
        device_id_type=MESH,
    )
    swap.start()
    plan_rows[...] = jnp.zeros_like(plan_rows)
    count = merge_ref.shape[1]
    ids = lax.broadcasted_iota(jnp.int32, (count, count), 0).astype(F32)
    lanes = lax.broadcasted_iota(jnp.int32, (count, count), 1).astype(F32)
    across = jnp.broadcast_to(merge_ref[0:1, :].astype(F32), (count, count))
    down_way = jnp.sum(jnp.where(ids == lanes, across, 0.0), axis=1, keepdims=True)
    before = (across < down_way) | ((across == down_way) & (lanes < ids))
    rank = jnp.sum(jnp.where(before, 1.0, 0.0), axis=1, keepdims=True)
    here_rank = rank == lanes
    after_rank = rank == lanes - 1.0
    listed = jnp.sum(jnp.where(here_rank, ids, 0.0), axis=0, keepdims=True)
    own_group = jnp.sum(jnp.where(here_rank, down_way, 0.0), axis=0, keepdims=True)
    last_group = jnp.sum(jnp.where(after_rank, down_way + 1.0, 0.0), axis=0, keepdims=True) - 1.0
    keep = jnp.where(own_group == last_group, 1.0, 0.0)
    ends = jnp.sum(jnp.where(down_way <= lanes, 1.0, 0.0), axis=0, keepdims=True) - 1.0
    for i, row in enumerate((listed, keep, ends)):
        plan_rows[i : i + 1, 0:count] = row.astype(jnp.int32)
    plan_copy = pltpu.make_async_copy(plan_rows, plan_ref, plan_sem)
    plan_copy.start()


    rows = lax.broadcasted_iota(jnp.int32, (NB, NB), 0)
    lanes = lax.broadcasted_iota(jnp.int32, (NB, NB), 1)
    same = rows == lanes

    swap.wait_recv()
    for b in range(blocks):
        selector = (rows == perm_ref[0:1, b * NB : (b + 1) * NB] - (z * units + b * NB)).astype(F32).astype(BF16)
        summed = part_ref[core, b] + inbox[b]
        turned = dot_exact(summed, selector, False, 0)
        gram_ref[b, x, y, core] = dot_exact(turned, selector, True, 1)

    rings = ("xy", "yx")
    ring_tasks = {}
    for b in range(blocks):
        for stage in range(2):
            pieces = (None,) if stage == 0 else tuple(offsets(XN))
            for index, piece in enumerate(pieces):
                for step, ways in ((1, (0, 1)), (2, last_ways(stage, b, XN, index))):
                    for way in ways:
                        ring_tasks[b, stage, way, step, piece] = len(ring_tasks)

    def ring_ref(b, stage, offset, piece):
        first, second = rings[b]
        at = dict(here)
        if stage == 0:
            at[first] = shifted(first, offset)
        else:
            at[first], at[second] = shifted(first, piece), shifted(second, offset)
        return gram_ref.at[b, at["x"], at["y"], core]

    ringed = {}

    def ring_start(b, stage, step, piece=None):
        for way in (0, 1):
            key = (b, stage, way, step, piece)
            if key not in ring_tasks:
                continue
            sign = 1 - 2 * way
            ref = ring_ref(b, stage, -sign * (step - 1), piece)
            copy = pltpu.make_async_remote_copy(
                src_ref=ref,
                dst_ref=ref,
                send_sem=ring_send.at[ring_tasks[key]],
                recv_sem=ring_recv.at[ring_tasks[key]],
                device_id=device(rings[b][stage], sign),
                device_id_type=MESH,
            )
            copy.start()
            ringed[key] = copy

    def ring_arrive(b, stage, step, piece=None):
        for way in (0, 1):
            key = (b, stage, way, step, piece)
            if key in ringed:
                ringed[key].wait_recv()

    relays = []

    def relay(b, offset):
        first, second = rings[b]
        pos = shifted(second, offset)
        ref = gram_ref.at[b, :, pos, core] if first == "x" else gram_ref.at[b, pos, :, core]
        copy = pltpu.make_async_remote_copy(
            src_ref=ref,
            dst_ref=ref,
            send_sem=relay_send.at[b, offset % XN],
            recv_sem=relay_recv.at[b, offset % XN],
            device_id=partner,
            device_id_type=MESH,
        )
        copy.start()
        relays.append(copy)

    both = range(blocks)
    for b in both:
        ring_start(b, 0, 1)
    for b in both:
        ring_start(b, 1, 1, 0)
    for b in both:
        ring_arrive(b, 0, 1)
        ring_start(b, 0, 2)
        ring_start(b, 1, 1, -1)
        ring_start(b, 1, 1, 1)
    for b in both:
        ring_arrive(b, 1, 1, 0)
        ring_start(b, 1, 2, 0)
    for b in both:
        ring_arrive(b, 0, 2)
        ring_start(b, 1, 1, 2)
        relay(b, 0)
    for b in both:
        for piece in (-1, 1, 2):
            ring_arrive(b, 1, 1, piece)
            ring_start(b, 1, 2, piece)
    spread_some(range(EARLY, len(others)))
    own_rows = pltpu.make_async_copy(moved.at[expert], spread.at[expert], keep_sem)
    own_rows.start()
    for b in both:
        relay(b, -1)
        relay(b, 1)
    for b in both:
        for piece in offsets(XN):
            ring_arrive(b, 1, 2, piece)
        relay(b, 2)
    for copy in relays:
        copy.wait_recv()
    plan_copy.wait()

    def listed_at(i, j):
        return jnp.minimum(jnp.maximum(plan_ref[i, j], 0), experts - 1)

    def gram_of(b, e):
        return gram_ref[b, lax.div(e, 2 * YN), lax.rem(lax.div(e, 2), YN), lax.rem(e, 2)]

    for b in range(blocks):

        def add_grams(i, run):
            for d in range(BATCH):
                j = i * BATCH + d
                run = run * plan_ref[1, j].astype(F32) + gram_of(b, listed_at(0, j))
                runs[j, 0:NB, :] = run
            return run

        lax.fori_loop(0, experts // BATCH, add_grams, jnp.zeros((NB, NB), F32))
        for m in range(MGROUPS):
            summed = runs[listed_at(2, m), 0:NB, :]
            diagonal = jnp.where(same, summed + RIDGE, 0.0)
            across = lax.rsqrt(jnp.sum(diagonal, axis=0, keepdims=True))
            down = lax.rsqrt(jnp.sum(diagonal, axis=1, keepdims=True))
            i = m * blocks + b
            scales[i] = jnp.broadcast_to(across, (8, NB))
            state[i] = jnp.where(same, diagonal, OFF_WEIGHT * summed) * down * across

    regroup(state, lanes)
    eliminate(state, rows, lanes)
    regroup(state, lanes)

    own_rows.wait()
    for copy in spreads:
        copy.wait_recv()

    for b in range(blocks):

        def add_terms(i, run):
            made = []
            for d in range(BATCH):
                e = listed_at(0, i * BATCH + d)
                high, low = split_two(gram_of(b, e))
                moved = spread[e, b]
                made.append(
                    jnp.dot(
                        jnp.concatenate([moved, moved], axis=1),
                        jnp.concatenate([high, low], axis=0),
                        preferred_element_type=F32,
                    )
                )
            for d in range(BATCH):
                run = run * plan_ref[1, i * BATCH + d].astype(F32) + made[d]
                runs[i * BATCH + d] = run
            return run

        lax.fori_loop(0, experts // BATCH, add_terms, jnp.zeros(runs.shape[1:], F32))
        for m in range(MGROUPS):
            terms[m * blocks + b] = runs[listed_at(2, m)]

    turn_rows = (rows & (LOW - 1)) * HIGH + lax.shift_right_logical(rows, 4)
    turn_lanes = (lanes & (LOW - 1)) * HIGH + lax.shift_right_logical(lanes, 4)
    earlier = turn_rows < turn_lanes
    for m in range(MGROUPS):
        for b in range(blocks):
            i = m * blocks + b
            full = state[i]
            lower = jnp.where(earlier, full, jnp.where(same, 1.0, 0.0))
            inverse = 1.0 / jnp.sum(jnp.where(same, full, 0.0), axis=0, keepdims=True)
            scale = scales[i, 0:1, :]
            half = dot3(terms[i] * scale, lower, 0) * inverse
            merged = dot3(half, lower, 1) * scale
            out_ref[m, :, b * NB : (b + 1) * NB] = merged.astype(BF16)

    for copy in relays + spreads + sent + list(ringed.values()) + list(started.values()):
        copy.wait_send()
    swap.wait_send()


def merge(tokens, routes, gate_weight, up_weight, down_weight, neuron_perm, merge_group):
    rows, width = tokens.shape
    units = gate_weight.shape[1]
    blocks = units // NB
    experts = merge_group.shape[0]
    columns = width // experts
    systems = MGROUPS * blocks
    listed = jnp.pad(routes.astype(BF16), ((0, 0), (0, NB - routes.shape[1])), constant_values=-1)
    wide = jnp.concatenate([tokens, listed], axis=1)
    part = (width + NB) // 3
    number = len(transfers())
    moved_shape = (experts, blocks, columns, NB)
    dma = pltpu.SemaphoreType.DMA
    return pl.pallas_call(
        partial(merge_kernel, part, width),
        out_shape=jax.ShapeDtypeStruct((MGROUPS, columns, units), BF16),
        in_specs=[pl.BlockSpec(memory_space=pl.ANY)] * 4 + [pl.BlockSpec(memory_space=pltpu.VMEM)] * 2,
        out_specs=pl.BlockSpec(memory_space=pltpu.VMEM),
        scratch_shapes=[
            pltpu.VMEM((XN, YN, ZN, 8, part), BF16),
            pltpu.VMEM((YN, XN, ZN, 8, part), BF16),
            pltpu.VMEM((ZN, XN, YN, 8, part), BF16),
            pltpu.VMEM((4, width, units), BF16),
            pltpu.VMEM((4, XN, YN, ZN, 8, units), F32),
            pltpu.VMEM((256, part), BF16),
            pltpu.VMEM((units, width), BF16),
            pltpu.VMEM(moved_shape, BF16),
            pltpu.VMEM((2, blocks, NB, NB), F32),
            pltpu.VMEM((8, NB), jnp.int32),
            pltpu.SMEM((8, NB), jnp.int32),
            pltpu.VMEM((blocks, XN, YN, 2, NB, NB), F32),
            pltpu.VMEM((blocks, NB, NB), F32),
            pltpu.VMEM(moved_shape, BF16),
            pltpu.VMEM((experts, columns, NB), F32),
            pltpu.VMEM((systems, NB, NB), F32),
            pltpu.VMEM((systems, columns, NB), F32),
            pltpu.VMEM((systems, 8, NB), F32),
            dma((number,)),
            dma((number,)),
            dma((3,)),
            dma((2,)),
            dma((2,)),
            dma((2,)),
            dma,
            dma,
            dma((blocks * 15,)),
            dma((blocks * 15,)),
            dma((blocks, XN)),
            dma((blocks, XN)),
            dma((2,)),
            dma((experts - 1,)),
            dma((experts - 1,)),
            dma,
        ],
        compiler_params=pltpu.CompilerParams(collective_id=0, has_side_effects=True, vmem_limit_bytes=62 * 1024 * 1024),
        name="merge",
    )(wide, gate_weight, up_weight, down_weight, neuron_perm, merge_group[None, :])


def per_device(tokens, routes, gate_weight, up_weight, down_weight, merge_group, neuron_perm):
    merged = merge(tokens, routes, gate_weight[0], up_weight[0], down_weight[0], neuron_perm, merge_group)
    return jnp.swapaxes(merged, 1, 2)


def solution(mesh):
    in_specs = (
        P(("expert", "group"), None),
        P(("expert", "group"), None),
        P("expert", None, "group"),
        P("expert", None, "group"),
        P("expert", "group", None),
        P(),
        P("expert", "group"),
    )
    return jax.shard_map(
        per_device, mesh=mesh, in_specs=in_specs, out_specs=P(None, "group", "expert"), check_vma=False
    )
```

```python
from functools import partial

import jax
import jax.numpy as jnp
from jax import lax
from jax.experimental import pallas as pl
from jax.experimental.pallas import tpu as pltpu
from jax.sharding import PartitionSpec as P

NB = 128
F32 = jnp.float32
BF16 = jnp.bfloat16
MESH = pl.DeviceIdType.MESH
XN, YN, ZN = 4, 4, 8
SIZES = {"x": XN, "y": YN, "z": ZN}
ORDERS = ("zyx", "zxy", "yxz")


def place(x, y, core):
    return (x * YN + y) * 2 + core


def offsets(n):
    listed = [0]
    for d in range(1, n // 2):
        listed += [-d, d]
    return listed + [n // 2]


def last_ways(stage, color, n, index):
    if stage == 0:
        return (color % 2,)
    return ((0, 1, 1, 0)[index % 4],)


def transfers():
    found = {}
    for color, order in enumerate(ORDERS):
        for stage, axis in enumerate(order):
            n = SIZES[axis]
            pieces = (None,) if stage == 0 else tuple(offsets(SIZES[order[stage - 1]]))
            for step in range(1, n // 2 + 1):
                for index, piece in enumerate(pieces):
                    ways = (0, 1) if step < n // 2 else last_ways(stage, color, n, index)
                    for way in ways:
                        found[color, stage, way, step, piece] = None
    return found


def arrivals(tasks, color, stage, offset):
    if offset == 0:
        if stage == 0:
            return set()
        below = SIZES[ORDERS[color][stage - 1]]
        return set().union(*(arrivals(tasks, color, stage - 1, d) for d in offsets(below)))
    return {
        t for t in tasks
        if t[0] == color and t[1] == stage and t[3] == abs(offset)
        and (abs(offset) == SIZES[ORDERS[color][stage]] // 2 or t[2] == (0 if offset < 0 else 1))
    }


def schedule(chunks, depth=4.0, shallow=-0.5):
    tasks = transfers()
    needs = {}
    for t in tasks:
        color, stage, way, step, piece = t
        if step > 1:
            needs[t] = {(color, stage, way, step - 1, piece)}
        else:
            needs[t] = arrivals(tasks, color, stage - 1, piece) if stage else set()
    takes = {}
    for color, order in enumerate(ORDERS):
        for d in offsets(SIZES[order[2]]):
            takes["take", color, d] = arrivals(tasks, color, 2, d)
    fill = [("chunk", i) for i in range(chunks)]
    rate, delay = 39e-3 / 0.047, 2.0
    now, busy, landed, waited, plan = 0.0, {}, {}, set(), []

    def flush(need):
        for t in sorted(need - waited, key=lambda t: landed[t]):
            plan.append(("wait", t))
            waited.add(t)

    def urgency(t):
        return (t[1], t[3], 0 if t[4] is None else abs(t[4]), t[0], t[2])

    todo = sorted(tasks, key=urgency)
    while todo or takes:
        ready = [t for t in todo if all(landed.get(d, 1e9) <= now for d in needs[t])]
        queue = []
        for t in ready:
            color, stage, way, step, piece = t
            link = (ORDERS[color][stage], way)
            size = 1 if stage < 2 else SIZES[ORDERS[color][0]]
            urgent = any(u[1] < 2 and (ORDERS[u[0]][u[1]], u[2]) == link for u in todo)
            if stage == 2 and busy.get(link, 0.0) - now > (shallow if urgent else depth):
                continue
            busy[link] = max(busy.get(link, 0.0), now) + size * rate
            landed[t] = busy[link] + delay
            queue.append(t)
        for t in queue:
            flush(needs[t])
            plan.append(("start", t))
            todo.remove(t)
        if queue:
            continue
        open_takes = [k for k in takes if all(landed.get(d, 1e9) <= now for d in takes[k])] if now > 16 else []
        if open_takes:
            key = open_takes[0]
            flush(takes.pop(key))
            plan.append(key)
            now += 1.4 if key[1] < 2 else 1.0
        elif fill and now > 8:
            plan.append(fill.pop(0))
            now += 0.7
        else:
            later = [v for v in landed.values() if v > now] + ([16.001] if now <= 16 else [])
            now = min(later) if later else now + 0.5
    return plan + fill


MGROUPS = 8
OFF_WEIGHT = 0.75
RIDGE = 1e-05
LOW = 16
BATCH = 4
EARLY = 13
HIGH = NB // LOW


def split_two(value):
    high = value.astype(BF16)
    return high, (value - high.astype(F32)).astype(BF16)


def dot3(left, right, contract):
    lh, ll = split_two(left)
    rh, rl = split_two(right)
    dims = (((1,), (contract,)), ((), ()))
    part = partial(lax.dot_general, dimension_numbers=dims, preferred_element_type=F32)
    return part(lh, rh) + part(lh, rl) + part(ll, rh)


def dot_exact(value, one_hot, value_left, contract):
    first = value.astype(BF16)
    rest = value - first.astype(F32)
    second = rest.astype(BF16)
    third = (rest - second.astype(F32)).astype(BF16)
    dims = (((contract,), (0,)), ((), ())) if value_left else (((0,), (contract,)), ((), ()))
    total = None
    for part in (first, second, third):
        pair = (part, one_hot) if value_left else (one_hot, part)
        term = lax.dot_general(*pair, dims, preferred_element_type=F32)
        total = term if total is None else total + term
    return total


def regroup(state, lanes):
    for bit in (1, 2, 4, 8):
        low = (lanes & bit) == 0
        for m in range(LOW):
            if m & bit:
                continue
            first, second = state[m], state[m | bit]
            state[m] = jnp.where(low, first, pltpu.roll(second, bit, 1))
            state[m | bit] = jnp.where(low, pltpu.roll(first, NB - bit, 1), second)


def eliminate(state, rows, lanes):
    def prepare(q, g):
        k = g * LOW + q
        pick = g * LOW + (lanes & (LOW - 1))
        row = jnp.take_along_axis(state[q], pick, axis=1, mode="promise_in_bounds")
        at_pivot = jnp.broadcast_to(state[q, pl.ds(k, 1), :], (8, NB))
        pivot = jnp.take_along_axis(at_pivot, pick[0:8], axis=1, mode="promise_in_bounds")
        inverse = (1.0 / pivot)[0:1]
        return (row + (rows == k).astype(F32)) * inverse

    for q in range(LOW):

        def step(g, scaled):
            k = g * LOW + q
            column = state[q, pl.ds(k, 1), :]
            column = jnp.where(lanes[0:1] >= (g + 1) * LOW, column, 0.0)
            state[q] = state[q] - column * scaled
            following = prepare(q, jnp.minimum(g + 1, HIGH - 1))
            for later in range(q + 1, LOW):
                state[later] = state[later] - state[later, pl.ds(k, 1), :] * scaled
            return following

        lax.fori_loop(0, HIGH, step, prepare(q, 0))


def merge_kernel(part, width, tok_ref, gate_ref, up_ref, down_ref, perm_ref, merge_ref, out_ref,
                 bufx, bufy, bufz, weights, acc, lhs, down, moved, part_ref, plan_rows, plan_ref,
                 gram_ref, inbox, spread, runs, state, terms, scales,
                 send_sem, recv_sem, own_sem, wsem, wsend, wrecv, dsem, plan_sem,
                 ring_send, ring_recv, relay_send, relay_recv, pair_sem, all_send, all_recv, keep_sem):
    expert = lax.axis_index("expert")
    z = lax.axis_index("group")
    core = lax.rem(expert, 2)
    y = lax.rem(lax.div(expert, 2), YN)
    x = lax.div(expert, 2 * YN)
    here = {"x": x, "y": y, "z": z}
    units = gate_ref.shape[1]
    blocks = units // NB
    experts = moved.shape[0]
    per_chunk = 4
    chunks = experts // per_chunk

    def shifted(axis, shift):
        return lax.rem(here[axis] + SIZES[axis] + shift, SIZES[axis])

    def device(axis, shift):
        at = dict(here)
        at[axis] = shifted(axis, shift)
        return (place(at["x"], at["y"], core), at["z"])

    partner = (place(x, y, 1 - core), z)
    bufs = (bufx, bufy, bufz)
    columns = (0, part, 2 * part)

    load_down = pltpu.make_async_copy(down_ref, down, dsem)
    load_down.start()
    barrier = pltpu.get_barrier_semaphore()
    others = [(dx, dy, dc) for dx in range(XN) for dy in range(YN) for dc in range(2) if dx or dy or dc]
    others = [others[(i * 13) % len(others)] for i in range(len(others))]

    def other(dx, dy, dc):
        return place(lax.rem(x + dx, XN), lax.rem(y + dy, YN), lax.rem(core + dc, 2))

    neighbours = [device("z", s) for s in (1, -1)] + [(other(*shift), z) for shift in others]
    for to in neighbours:
        pl.semaphore_signal(barrier, inc=1, device_id=to, device_id_type=MESH)
    pl.semaphore_wait(barrier, len(neighbours))

    numbers = {t: i for i, t in enumerate(transfers())}

    def piece_ref(color, stage, offset, piece):
        order = ORDERS[color]
        buf = bufs[color]
        if stage == 0:
            return buf.at[here[order[2]], here[order[1]], shifted(order[0], offset)]
        if stage == 1:
            return buf.at[here[order[2]], shifted(order[1], offset), shifted(order[0], piece)]
        return buf.at[shifted(order[2], offset), shifted(order[1], piece)]

    started = {}

    def start(task):
        color, stage, way, step, piece = task
        sign = 1 - 2 * way
        dst = piece_ref(color, stage, -sign * (step - 1), piece)
        first = step == 1 and (stage == 0 or (stage == 1 and piece == 0))
        src = tok_ref.at[:, pl.ds(columns[color], part)] if first else dst
        i = numbers[task]
        copy = pltpu.make_async_remote_copy(
            src_ref=src,
            dst_ref=dst,
            send_sem=send_sem.at[i],
            recv_sem=recv_sem.at[i],
            device_id=device(ORDERS[color][stage], sign),
            device_id_type=MESH,
        )
        copy.start()
        started[task] = copy

    own = []
    for color in range(3):
        copy = pltpu.make_async_copy(
            tok_ref.at[:, pl.ds(columns[color], part)], piece_ref(color, 0, 0, None), own_sem.at[color]
        )
        copy.start()
        own.append(copy)
    moves = []

    def move_weights():
        for j, ref in enumerate((gate_ref, up_ref)):
            local = pltpu.make_async_copy(ref, weights.at[core * 2 + j], wsem.at[j])
            local.start()
            remote = pltpu.make_async_remote_copy(
                src_ref=ref,
                dst_ref=weights.at[core * 2 + j],
                send_sem=wsend.at[j],
                recv_sem=wrecv.at[j],
                device_id=partner,
                device_id_type=MESH,
            )
            remote.start()
            moves.append((local, remote))

    def multiply(rows, depth, first_row, color, plane):
        def per_column(n, carry):
            w = weights[n, pl.ds(first_row, depth), :]
            value = jnp.dot(lhs[0:rows, 0:depth], w, preferred_element_type=F32)
            if color == 0:
                acc[n, plane] += value.reshape(YN, ZN, 8, units)
            elif color == 1:
                acc[n, :, plane] += value.reshape(XN, ZN, 8, units)
            else:
                acc[n, :, :, plane] += value.reshape(XN, YN, 8, units)
            return carry

        lax.fori_loop(0, 4, per_column, 0)

    def take(color, offset):
        plane = shifted(ORDERS[color][2], offset)
        depth = part if color < 2 else width - 2 * part
        rows = 256 if color < 2 else 128
        value = bufs[color][plane, :, :, :, 0:depth].astype(F32)
        lhs[0:rows, 0:depth] = value.reshape(rows, depth).astype(BF16)
        multiply(rows, depth, columns[color], color, plane)

    unit_rows = lax.broadcasted_iota(jnp.int32, (NB, NB), 0)
    span = per_chunk * (width // experts)

    def chunk(i):
        for b in range(blocks):
            within = perm_ref[0:1, b * NB : (b + 1) * NB] - (z * units + b * NB)
            selector = (unit_rows == within).astype(F32).astype(BF16)
            piece = down[b * NB : (b + 1) * NB, i * span : (i + 1) * span]
            turned = lax.dot_general(piece, selector, (((0,), (0,)), ((), ())), preferred_element_type=F32)
            moved[i * per_chunk : (i + 1) * per_chunk, b] = turned.astype(BF16).reshape(per_chunk, span // per_chunk, NB)

    spreads = []

    def spread_some(which):
        for i in which:
            to = other(*others[i])
            copy = pltpu.make_async_remote_copy(
                src_ref=moved.at[to],
                dst_ref=spread.at[expert],
                send_sem=all_send.at[i],
                recv_sem=all_recv.at[i],
                device_id=(to, z),
                device_id_type=MESH,
            )
            copy.start()
            spreads.append(copy)

    order = schedule(chunks)
    starts_left = len(numbers)
    begun = False
    settled = False
    for action, *rest in order:
        if action == "start":
            if not settled and rest[0][1] > 0:
                for copy in own:
                    copy.wait()
                settled = True
            start(rest[0])
            starts_left -= 1
            if starts_left == 0:
                spread_some(range(EARLY))
        elif not begun:
            move_weights()
            acc[...] = jnp.zeros_like(acc)
            begun = True
        if action == "wait":
            started[rest[0]].wait_recv()
        elif action == "chunk":
            if rest[0] == 0:
                load_down.wait()
            chunk(rest[0])
        elif action == "take":
            if moves[0] is not None:
                for local, remote in moves:
                    local.wait()
                    remote.wait_recv()
                sent = [remote for _, remote in moves]
                moves[0] = None
            take(*rest)

    part_ref[...] = jnp.zeros_like(part_ref)
    spare = width - 2 * part

    def finish(i, carry):
        px, p = lax.rem(i, XN), lax.rem(1 - core + lax.div(i, XN), 2)
        named = (place(x, y, 0) + p).astype(F32)
        gate = acc[2 * p, px].reshape(256, units)
        up = acc[2 * p + 1, px].reshape(256, units)
        listed = jnp.concatenate(
            [bufz[:, px, py, :, spare : spare + NB].astype(F32).reshape(ZN * 8, NB) for py in range(YN)], axis=0
        )
        chosen = jnp.max(jnp.where(listed == named, 1.0, 0.0), axis=1, keepdims=True)
        value = gate / (1.0 + jnp.exp(-gate)) * up
        hidden = jnp.where(chosen > 0.5, value, 0.0).astype(BF16)
        for b in range(blocks):
            piece = hidden[:, b * NB : (b + 1) * NB]
            part_ref[p, b] += lax.dot_general(piece, piece, (((0,), (0,)), ((), ())), preferred_element_type=F32)
        return carry

    lax.fori_loop(0, 2 * XN, finish, 0)
    swap = pltpu.make_async_remote_copy(
        src_ref=part_ref.at[1 - core],
        dst_ref=inbox,
        send_sem=pair_sem.at[0],
        recv_sem=pair_sem.at[1],
        device_id=partner,
        device_id_type=MESH,
    )
    swap.start()
    plan_rows[...] = jnp.zeros_like(plan_rows)
    count = merge_ref.shape[1]
    ids = lax.broadcasted_iota(jnp.int32, (count, count), 0).astype(F32)
    lanes = lax.broadcasted_iota(jnp.int32, (count, count), 1).astype(F32)
    across = jnp.broadcast_to(merge_ref[0:1, :].astype(F32), (count, count))
    down_way = jnp.sum(jnp.where(ids == lanes, across, 0.0), axis=1, keepdims=True)
    before = (across < down_way) | ((across == down_way) & (lanes < ids))
    rank = jnp.sum(jnp.where(before, 1.0, 0.0), axis=1, keepdims=True)
    here_rank = rank == lanes
    after_rank = rank == lanes - 1.0
    listed = jnp.sum(jnp.where(here_rank, ids, 0.0), axis=0, keepdims=True)
    own_group = jnp.sum(jnp.where(here_rank, down_way, 0.0), axis=0, keepdims=True)
    last_group = jnp.sum(jnp.where(after_rank, down_way + 1.0, 0.0), axis=0, keepdims=True) - 1.0
    keep = jnp.where(own_group == last_group, 1.0, 0.0)
    ends = jnp.sum(jnp.where(down_way <= lanes, 1.0, 0.0), axis=0, keepdims=True) - 1.0
    for i, row in enumerate((listed, keep, ends)):
        plan_rows[i : i + 1, 0:count] = row.astype(jnp.int32)
    plan_copy = pltpu.make_async_copy(plan_rows, plan_ref, plan_sem)
    plan_copy.start()


    rows = lax.broadcasted_iota(jnp.int32, (NB, NB), 0)
    lanes = lax.broadcasted_iota(jnp.int32, (NB, NB), 1)
    same = rows == lanes

    swap.wait_recv()
    for b in range(blocks):
        selector = (rows == perm_ref[0:1, b * NB : (b + 1) * NB] - (z * units + b * NB)).astype(F32).astype(BF16)
        summed = part_ref[core, b] + inbox[b]
        turned = dot_exact(summed, selector, False, 0)
        gram_ref[b, x, y, core] = dot_exact(turned, selector, True, 1)

    rings = ("xy", "yx")
    ring_tasks = {}
    for b in range(blocks):
        for stage in range(2):
            pieces = (None,) if stage == 0 else tuple(offsets(XN))
            for index, piece in enumerate(pieces):
                for step, ways in ((1, (0, 1)), (2, last_ways(stage, b, XN, index))):
                    for way in ways:
                        ring_tasks[b, stage, way, step, piece] = len(ring_tasks)

    def ring_ref(b, stage, offset, piece):
        first, second = rings[b]
        at = dict(here)
        if stage == 0:
            at[first] = shifted(first, offset)
        else:
            at[first], at[second] = shifted(first, piece), shifted(second, offset)
        return gram_ref.at[b, at["x"], at["y"], core]

    ringed = {}

    def ring_start(b, stage, step, piece=None):
        for way in (0, 1):
            key = (b, stage, way, step, piece)
            if key not in ring_tasks:
                continue
            sign = 1 - 2 * way
            ref = ring_ref(b, stage, -sign * (step - 1), piece)
            copy = pltpu.make_async_remote_copy(
                src_ref=ref,
                dst_ref=ref,
                send_sem=ring_send.at[ring_tasks[key]],
                recv_sem=ring_recv.at[ring_tasks[key]],
                device_id=device(rings[b][stage], sign),
                device_id_type=MESH,
            )
            copy.start()
            ringed[key] = copy

    def ring_arrive(b, stage, step, piece=None):
        for way in (0, 1):
            key = (b, stage, way, step, piece)
            if key in ringed:
                ringed[key].wait_recv()

    relays = []

    def relay(b, offset):
        first, second = rings[b]
        pos = shifted(second, offset)
        ref = gram_ref.at[b, :, pos, core] if first == "x" else gram_ref.at[b, pos, :, core]
        copy = pltpu.make_async_remote_copy(
            src_ref=ref,
            dst_ref=ref,
            send_sem=relay_send.at[b, offset % XN],
            recv_sem=relay_recv.at[b, offset % XN],
            device_id=partner,
            device_id_type=MESH,
        )
        copy.start()
        relays.append(copy)

    both = range(blocks)
    for b in both:
        ring_start(b, 0, 1)
    for b in both:
        ring_start(b, 1, 1, 0)
    for b in both:
        ring_arrive(b, 0, 1)
        ring_start(b, 0, 2)
        ring_start(b, 1, 1, -1)
        ring_start(b, 1, 1, 1)
    for b in both:
        ring_arrive(b, 1, 1, 0)
        ring_start(b, 1, 2, 0)
    for b in both:
        ring_arrive(b, 0, 2)
        ring_start(b, 1, 1, 2)
        relay(b, 0)
    for b in both:
        for piece in (-1, 1, 2):
            ring_arrive(b, 1, 1, piece)
            ring_start(b, 1, 2, piece)
    spread_some(range(EARLY, len(others)))
    own_rows = pltpu.make_async_copy(moved.at[expert], spread.at[expert], keep_sem)
    own_rows.start()
    for b in both:
        relay(b, -1)
        relay(b, 1)
    for b in both:
        for piece in offsets(XN):
            ring_arrive(b, 1, 2, piece)
        relay(b, 2)
    for copy in relays:
        copy.wait_recv()
    plan_copy.wait()

    def listed_at(i, j):
        return jnp.minimum(jnp.maximum(plan_ref[i, j], 0), experts - 1)

    def gram_of(b, e):
        return gram_ref[b, lax.div(e, 2 * YN), lax.rem(lax.div(e, 2), YN), lax.rem(e, 2)]

    for b in range(blocks):

        def add_grams(i, run):
            for d in range(BATCH):
                j = i * BATCH + d
                run = run * plan_ref[1, j].astype(F32) + gram_of(b, listed_at(0, j))
                runs[j, 0:NB, :] = run
            return run

        lax.fori_loop(0, experts // BATCH, add_grams, jnp.zeros((NB, NB), F32))
        for m in range(MGROUPS):
            summed = runs[listed_at(2, m), 0:NB, :]
            diagonal = jnp.where(same, summed + RIDGE, 0.0)
            across = lax.rsqrt(jnp.sum(diagonal, axis=0, keepdims=True))
            down = lax.rsqrt(jnp.sum(diagonal, axis=1, keepdims=True))
            i = m * blocks + b
            scales[i] = jnp.broadcast_to(across, (8, NB))
            state[i] = jnp.where(same, diagonal, OFF_WEIGHT * summed) * down * across

    regroup(state, lanes)
    eliminate(state, rows, lanes)
    regroup(state, lanes)

    own_rows.wait()
    for copy in spreads:
        copy.wait_recv()

    for b in range(blocks):

        def add_terms(i, run):
            made = []
            for d in range(BATCH):
                e = listed_at(0, i * BATCH + d)
                high, low = split_two(gram_of(b, e))
                moved = spread[e, b]
                made.append(
                    jnp.dot(
                        jnp.concatenate([moved, moved], axis=1),
                        jnp.concatenate([high, low], axis=0),
                        preferred_element_type=F32,
                    )
                )
            for d in range(BATCH):
                run = run * plan_ref[1, i * BATCH + d].astype(F32) + made[d]
                runs[i * BATCH + d] = run
            return run

        lax.fori_loop(0, experts // BATCH, add_terms, jnp.zeros(runs.shape[1:], F32))
        for m in range(MGROUPS):
            terms[m * blocks + b] = runs[listed_at(2, m)]

    turn_rows = (rows & (LOW - 1)) * HIGH + lax.shift_right_logical(rows, 4)
    turn_lanes = (lanes & (LOW - 1)) * HIGH + lax.shift_right_logical(lanes, 4)
    earlier = turn_rows < turn_lanes
    for m in range(MGROUPS):
        for b in range(blocks):
            i = m * blocks + b
            full = state[i]
            lower = jnp.where(earlier, full, jnp.where(same, 1.0, 0.0))
            inverse = 1.0 / jnp.sum(jnp.where(same, full, 0.0), axis=0, keepdims=True)
            scale = scales[i, 0:1, :]
            half = dot3(terms[i] * scale, lower, 0) * inverse
            merged = dot3(half, lower, 1) * scale
            out_ref[m, :, b * NB : (b + 1) * NB] = merged.astype(BF16)

    for copy in relays + spreads + sent + list(ringed.values()) + list(started.values()):
        copy.wait_send()
    swap.wait_send()


def merge(tokens, routes, gate_weight, up_weight, down_weight, neuron_perm, merge_group):
    rows, width = tokens.shape
    units = gate_weight.shape[1]
    blocks = units // NB
    experts = merge_group.shape[0]
    columns = width // experts
    systems = MGROUPS * blocks
    listed = jnp.pad(routes.astype(BF16), ((0, 0), (0, NB - routes.shape[1])), constant_values=-1)
    wide = jnp.concatenate([tokens, listed], axis=1)
    part = (width + NB) // 3
    number = len(transfers())
    moved_shape = (experts, blocks, columns, NB)
    dma = pltpu.SemaphoreType.DMA
    return pl.pallas_call(
        partial(merge_kernel, part, width),
        out_shape=jax.ShapeDtypeStruct((MGROUPS, columns, units), BF16),
        in_specs=[pl.BlockSpec(memory_space=pl.ANY)] * 4 + [pl.BlockSpec(memory_space=pltpu.VMEM)] * 2,
        out_specs=pl.BlockSpec(memory_space=pltpu.VMEM),
        scratch_shapes=[
            pltpu.VMEM((XN, YN, ZN, 8, part), BF16),
            pltpu.VMEM((YN, XN, ZN, 8, part), BF16),
            pltpu.VMEM((ZN, XN, YN, 8, part), BF16),
            pltpu.VMEM((4, width, units), BF16),
            pltpu.VMEM((4, XN, YN, ZN, 8, units), F32),
            pltpu.VMEM((256, part), BF16),
            pltpu.VMEM((units, width), BF16),
            pltpu.VMEM(moved_shape, BF16),
            pltpu.VMEM((2, blocks, NB, NB), F32),
            pltpu.VMEM((8, NB), jnp.int32),
            pltpu.SMEM((8, NB), jnp.int32),
            pltpu.VMEM((blocks, XN, YN, 2, NB, NB), F32),
            pltpu.VMEM((blocks, NB, NB), F32),
            pltpu.VMEM(moved_shape, BF16),
            pltpu.VMEM((experts, columns, NB), F32),
            pltpu.VMEM((systems, NB, NB), F32),
            pltpu.VMEM((systems, columns, NB), F32),
            pltpu.VMEM((systems, 8, NB), F32),
            dma((number,)),
            dma((number,)),
            dma((3,)),
            dma((2,)),
            dma((2,)),
            dma((2,)),
            dma,
            dma,
            dma((blocks * 15,)),
            dma((blocks * 15,)),
            dma((blocks, XN)),
            dma((blocks, XN)),
            dma((2,)),
            dma((experts - 1,)),
            dma((experts - 1,)),
            dma,
        ],
        compiler_params=pltpu.CompilerParams(collective_id=0, has_side_effects=True, vmem_limit_bytes=62 * 1024 * 1024),
        name="merge",
    )(wide, gate_weight, up_weight, down_weight, neuron_perm, merge_group[None, :])


def per_device(tokens, routes, gate_weight, up_weight, down_weight, merge_group, neuron_perm):
    merged = merge(tokens, routes, gate_weight[0], up_weight[0], down_weight[0], neuron_perm, merge_group)
    return jnp.swapaxes(merged, 1, 2)


def solution(mesh):
    in_specs = (
        P(("expert", "group"), None),
        P(("expert", "group"), None),
        P("expert", None, "group"),
        P("expert", None, "group"),
        P("expert", "group", None),
        P(),
        P("expert", "group"),
    )
    return jax.shard_map(
        per_device, mesh=mesh, in_specs=in_specs, out_specs=P(None, "group", "expert"), check_vma=False
    )
```
